256 devices in a mesh: row: 8 (over y, x_hi), col: 32 (over z, x_lo, core).
Axes of the slice: x: 4 (x_hi: 2, x_lo: 2; x = x_hi * 2 + x_lo), y: 4, z: 8, core: 2. Of those that a mesh axis runs over, the one named last changes fastest.
Arguments:
- allele_doses: int32 [8192, 65536], P('row', 'col'), may hold values from 0 to 2
- disease_status: int32 [8192], P('row'), may hold values from 0 to 1
- walker_cloud: float32 [64, 65536], P(None, 'col'), may hold values from -21 to 21
- normal_perturbations: float32 [2, 64, 65536], P(None, None, 'col'), may hold values from -6 to 6
- approval_flags: int32 [2, 64], replicated, may hold values 0 or 1
- present_heat: float32 [1], replicated, may hold values from 0.85 to 0.92
- heat_advance: float32 [1], replicated, may hold values from 0.02 to 0.08
- drift_magnitude: float32 [1], replicated, may hold values from 0.8 to 1.2
Outputs:
- particles_out: float32 [64, 65536], P(None, 'col')
- log_weights: float32 [64], replicated
- mean_loglik: float32 [64], replicated
The draws below stay inside these ranges and needn't reach their ends.
All inputs are finite; a program needn't handle non-finite values.
Results may differ from the reference program's by a relative error of at most 0.0035.
Values may be sent and summed in bfloat16 or wider, within the bound.
A program may use at most 64 MiB of HBM per device.

```python
import math
import jax
import jax.numpy as jnp
from jax import lax

P_SIZE = 65536
K = 64
N = 8192
N_ROW = 8


def draw_walker_cloud(key, part):
    first, second = jax.random.split(jax.random.fold_in(key, 7301), 2)
    particle_location = jnp.arange(P_SIZE, dtype=jnp.float32) / float(P_SIZE - 1)
    column_scale = jnp.exp(jnp.log(3.0) * particle_location) * jax.random.uniform(second, (P_SIZE,), jnp.float32, 0.7, 1.4)
    base = jax.random.normal(first, (K, P_SIZE), jnp.float32)
    base = jnp.clip(base, -5.0, 5.0)
    return base * column_scale[None, :]


def plant(drawn, stream_key, least, top_value):
    extent = drawn.shape
    index_at = [jax.random.randint(jax.random.fold_in(stream_key, axis), (), 0, extent[axis]) for axis in range(len(extent))]
    drawn = drawn.at[tuple(index_at)].set(least)
    longest = extent.index(max(extent))
    index_at[longest] = (index_at[longest] + 1) % extent[longest]
    return drawn.at[tuple(index_at)].set(top_value)


def block_levels(own_key, extent, shards, smallest, high):
    gain = 1.0
    for axis_at, blocks in shards:
        steps = jax.random.uniform(jax.random.fold_in(jax.random.fold_in(own_key, 6), axis_at), (blocks,), jnp.float32, smallest / len(shards), high / len(shards))
        gain = gain * jnp.repeat(jnp.exp(steps), extent[axis_at] // blocks).reshape((-1,) + (1,) * (len(extent) - 1 - axis_at))
    return gain


def bell_draw(own_key, shape, deviation, limit, cuts=(), kind=jnp.bfloat16):
    values = jax.random.normal(own_key, shape, jnp.float32) * deviation
    if len(cuts) > 0:
        values = block_levels(own_key, shape, cuts, -0.22, 0.18) * values
    return jnp.clip(values, min=-limit, max=limit).astype(kind)


def setup_inputs(seed: int = 0) -> dict:
    keys = jax.random.split(jax.random.key(seed), 9)
    allele_doses = plant(jax.random.randint(keys[0], (N, P_SIZE), 0, 3), jax.random.fold_in(keys[0], 1), 0, 2).astype(jnp.int32)
    disease_status = plant(jax.random.randint(keys[1], (N,), 0, 2), jax.random.fold_in(keys[1], 1), 0, 1).astype(jnp.int32)
    walker_cloud = draw_walker_cloud(jax.random.fold_in(keys[8], 71), 0)
    normal_perturbations = bell_draw(keys[3], (2, K, P_SIZE), 1.0, 6.0, ((2, 32),), jnp.float32)
    approval_flags = plant((jax.random.randint(keys[4], (2, K), 0, 4) < 3).astype(jnp.int32), jax.random.fold_in(keys[4], 1), 0, 1)
    present_heat = jnp.clip(jax.random.uniform(keys[5], (1,), jnp.float32, 0.85, 0.92), 0.85, 0.92)
    heat_advance = jnp.clip(jnp.exp(jax.random.uniform(keys[6], (1,), jnp.float32, math.log(0.02), math.log(0.08))), 0.02, 0.08)
    drift_magnitude = jnp.clip(jnp.exp(jax.random.uniform(keys[7], (1,), jnp.float32, math.log(0.8), math.log(1.2))), 0.8, 1.2)
    return {"allele_doses": allele_doses, "disease_status": disease_status, "walker_cloud": walker_cloud, "normal_perturbations": normal_perturbations, "approval_flags": approval_flags, "present_heat": present_heat, "heat_advance": heat_advance, "drift_magnitude": drift_magnitude}


CLIP_FLOOR = 4.0
SHRINKAGE_LEVEL = 0.5

def logits_of(allele_doses, regression_weight):
    reciprocal_square = float(P_SIZE) ** (-0.5)
    coef_bf = regression_weight.astype(jnp.bfloat16)
    blocks = allele_doses.reshape(N_ROW, -1, P_SIZE)

    def single_block_result(block):
        centered = (block - 1).astype(jnp.bfloat16)
        return jnp.dot(centered, coef_bf.T, preferred_element_type=jnp.float32)
    return lax.map(single_block_result, blocks).reshape(-1, K) * reciprocal_square

def likgrad_of(allele_doses, residual_bf):
    blocks = allele_doses.reshape(N_ROW, -1, P_SIZE)
    residual_block_list = residual_bf.reshape(N_ROW, -1, K)

    def single_block_result(pair):
        centered = (pair[0] - 1).astype(jnp.bfloat16)
        partial_sum = jnp.dot(pair[1].T, centered, preferred_element_type=jnp.float32)
        rounded = lax.optimization_barrier(partial_sum.astype(jnp.bfloat16))
        return rounded.astype(jnp.float32)
    return lax.optimization_barrier(jnp.sum(lax.map(single_block_result, (blocks, residual_block_list)), axis=0))

def loglik_of(outcome, linear_predictor):
    return lax.optimization_barrier(jnp.sum(outcome[:, None] * linear_predictor - jax.nn.softplus(linear_predictor), axis=0))

def reference(allele_doses, disease_status, walker_cloud, normal_perturbations, approval_flags, present_heat, heat_advance, drift_magnitude):
    reciprocal_square = float(P_SIZE) ** (-0.5)
    outcome = disease_status.astype(jnp.float32)
    upcoming_heat = present_heat[0] + heat_advance[0]
    stepped = drift_magnitude[0]
    linear_predictor = logits_of(allele_doses, walker_cloud)
    loglik = loglik_of(outcome, linear_predictor)
    scaled = heat_advance[0] * loglik
    clipped = jnp.maximum(scaled - jnp.max(scaled), -CLIP_FLOOR)
    log_weights = clipped - jnp.log(jnp.sum(jnp.exp(clipped)))
    weights = jnp.exp(log_weights)
    center = lax.optimization_barrier(jnp.sum(weights[:, None] * walker_cloud, axis=0))
    spread = lax.optimization_barrier(jnp.sum(weights[:, None] * (walker_cloud - center[None, :]) ** 2, axis=0)) + 1e-06
    precond = spread / (jnp.sum(spread) / P_SIZE)
    regression_weight = walker_cloud
    for move in range(2):
        residual_bf = (outcome[:, None] - jax.nn.sigmoid(linear_predictor)).astype(jnp.bfloat16)
        fitness_slope = likgrad_of(allele_doses, residual_bf)
        slope_vector = upcoming_heat * reciprocal_square * fitness_slope - SHRINKAGE_LEVEL * regression_weight / jnp.sqrt(regression_weight * regression_weight + 1.0)
        proposal = regression_weight + stepped * precond[None, :] * slope_vector + jnp.sqrt(2.0 * stepped * precond)[None, :] * normal_perturbations[move]
        regression_weight = jnp.where(approval_flags[move][:, None] == 1, proposal, regression_weight)
        linear_predictor = logits_of(allele_doses, regression_weight)
    mean_loglik = loglik_of(outcome, linear_predictor) / (P_SIZE * 0 + allele_doses.shape[0])
    return (regression_weight, log_weights, mean_loglik)
```

```python
import jax
import jax.numpy as jnp
from jax import lax
from jax.experimental import pallas as pl
from jax.experimental.pallas import tpu as pltpu
from jax.sharding import Mesh
from jax.sharding import PartitionSpec as P

P_SIZE = 65536
K = 64
ROW = ("row_0", "row_1")
COL = ("col_0", "col_1", "col_2")
CLIP_FLOOR = 4.0
SHRINKAGE_LEVEL = 0.5
MESH = pl.DeviceIdType.MESH

ROWS = 1024
COLS = 2048
NZ, NQ, NT, NR = 8, 4, 32, 8
TP = 128
TK = 16
WR = COLS // NR
NMOVE = 2
ROW_OFFSETS = ((2, 1), (1, 1), (3, 1), (2, 0), (0, 1), (1, 0), (3, 0))


def kernel(
    x_hbm, y_ref, c_hbm, noise_hbm, flags_ref, heat_ref, adv_ref, drift_ref,
    out_hbm, lw_ref, ml_ref,
    xi, xb, c, noise, cb, base, spread, scale, rfull,
    pf, rf, ps, rs, resid, gsend, grecv, hfull,
    ll_send, ll_col, llr_send, llr, sp_send, sp_col,
    xsem, lsem, osem, ssem, rsem,
):
    f32, bf16 = jnp.float32, jnp.bfloat16
    y, xh = lax.axis_index("row_0"), lax.axis_index("row_1")
    z, xl, co = lax.axis_index("col_0"), lax.axis_index("col_1"), lax.axis_index("col_2")
    q = xl * 2 + co
    me = z * NQ + q
    rho = y * 2 + xh
    scale_s = float(P_SIZE) ** (-0.5)

    def z_at(k):
        off = 4 + (1 - 2 * lax.rem(k, 2)) * ((k + 1) // 2)
        return lax.rem(z + off, NZ)

    copy_c = pltpu.make_async_copy(c_hbm, c, lsem.at[0])
    copy_c.start()

    def x_copy(k):
        rows = pl.ds(pl.multiple_of(z_at(k) * TP, TP), TP)
        return pltpu.make_async_copy(x_hbm.at[rows], xi.at[k], xsem.at[k])

    @pl.loop(0, NZ)
    def _(k):
        x_copy(k).start()

    copy_noise = pltpu.make_async_copy(noise_hbm, noise, lsem.at[1])
    copy_noise.start()

    barrier = pltpu.get_barrier_semaphore()

    def col_id(d):
        return (y, xh, d // NQ, lax.rem(d // 2, 2), lax.rem(d, 2))

    def row_id(o):
        return (lax.rem(y + o[0], 4), lax.rem(xh + o[1], 2), z, xl, co)

    @pl.loop(1, NT)
    def _(r):
        pl.semaphore_signal(barrier, inc=1, device_id=col_id(lax.rem(me + r, NT)), device_id_type=MESH)

    for o in ROW_OFFSETS:
        pl.semaphore_signal(barrier, inc=1, device_id=row_id(o), device_id_type=MESH)

    def landed(ref, sem):
        pltpu.make_async_copy(ref, ref, sem).wait()

    def to_col(src, dst, sems, send_at, recv_at):
        @pl.loop(0, NZ)
        def _(k):
            zd = z_at(k)
            for qd in range(NQ):
                @pl.when(jnp.logical_or(zd != z, qd != q))
                def _():
                    pltpu.make_async_remote_copy(
                        src_ref=src, dst_ref=dst, send_sem=send_at, recv_sem=recv_at,
                        device_id=(y, xh, zd, qd // 2, qd % 2), device_id_type=MESH,
                    ).start()

    def to_row(src, dst, send_at, recv_at):
        for o in ROW_OFFSETS:
            pltpu.make_async_remote_copy(
                src_ref=src, dst_ref=dst, send_sem=send_at, recv_sem=recv_at,
                device_id=row_id(o), device_id_type=MESH,
            ).start()

    def logits_phase(t, sent, got, n):
        @pl.loop(0, NZ)
        def _(k):
            zd = z_at(k)
            rows = pl.ds(pl.multiple_of(zd * TP, TP), TP)
            if t == 0:
                x_copy(k).wait()
                xb[rows, :] = (xi[k].astype(f32) - 1.0).astype(bf16)
            part = lax.dot_general(
                cb[...], xb[rows, :], (((1,), (1,)), ((), ())), preferred_element_type=f32
            )
            for qd in range(NQ):
                sent[zd * NQ + qd] = part[qd * TK:(qd + 1) * TK, :].astype(sent.dtype)
            for qd in range(NQ):
                @pl.when(jnp.logical_or(zd != z, qd != q))
                def _():
                    pltpu.make_async_remote_copy(
                        src_ref=sent.at[zd * NQ + qd], dst_ref=got.at[me],
                        send_sem=ssem.at[n], recv_sem=rsem.at[n],
                        device_id=(y, xh, zd, qd // 2, qd % 2), device_id_type=MESH,
                    ).start()
        got[me] = sent[me]
        landed(got.at[pl.ds(0, NT - 1)], rsem.at[n])
        return jnp.sum(got[...].astype(f32), axis=0) * scale_s

    outcome = y_ref[pl.ds(z, 1), :].astype(f32)
    sub = lax.broadcasted_iota(jnp.int32, (TK, TP), 0)
    lane = lax.broadcasted_iota(jnp.int32, (TK, TP), 1)

    def loglik_row(tile):
        soft = jnp.maximum(tile, 0.0) + jnp.log1p(jnp.exp(-jnp.abs(tile)))
        total = jnp.sum(outcome * tile - soft, axis=1, keepdims=True)
        return jnp.sum(jnp.where(lane == sub + q * TK, total, 0.0), axis=0, keepdims=True)

    eye = lax.broadcasted_iota(jnp.int32, (K, TP), 0) == lax.broadcasted_iota(jnp.int32, (K, TP), 1)

    def as_column(row):
        return jnp.sum(jnp.where(eye, row, 0.0), axis=1, keepdims=True)

    flags = [
        as_column(flags_ref[t:t + 1, :].astype(f32)) > 0.5 for t in range(NMOVE)
    ]
    present = heat_ref[0]
    advance = adv_ref[0]
    stepped = drift_ref[0]
    upcoming = present + advance

    copy_c.wait()
    cb[...] = c[...].astype(bf16)
    pl.semaphore_wait(barrier, NT - 1 + NR - 1)
    tile = logits_phase(0, pf, rf, 0)

    def loglik_send(u, tile):
        ll_send[u] = loglik_row(tile)
        ll_col[u, me] = ll_send[u]
        to_col(ll_send.at[u], ll_col.at[u, me], None, ssem.at[10 + u], rsem.at[10 + u])

    def loglik_over_col(u):
        landed(ll_col.at[u, pl.ds(0, NT - 1)], rsem.at[10 + u])
        llr_send[u] = jnp.sum(ll_col[u], axis=0)
        llr[u, rho] = llr_send[u]
        to_row(llr_send.at[u], llr.at[u, rho], ssem.at[12 + u], rsem.at[12 + u])

    def loglik_total(u):
        landed(llr.at[u, pl.ds(0, NR - 1)], rsem.at[12 + u])
        return jnp.sum(llr[u], axis=0)

    copy_noise.wait()
    for t in range(NMOVE):
        resid[t, me] = (outcome - jax.nn.sigmoid(tile)).astype(bf16)
        to_col(resid.at[t, me], resid.at[t, me], None, ssem.at[3 + t], rsem.at[3 + t])
        if t == 0:
            loglik_send(0, tile)
        landed(resid.at[t, pl.ds(0, NT - 1)], rsem.at[3 + t])
        for p in range(NZ):
            rfull[:, p * TP:(p + 1) * TP] = resid[t, p * NQ:(p + 1) * NQ].reshape(K, TP)

        def share(d):
            cols = pl.ds(pl.multiple_of(d * WR, WR), WR)
            return jnp.dot(rfull[...], xb[:, cols], preferred_element_type=f32).astype(bf16)

        for o in ROW_OFFSETS:
            ident = row_id(o)
            d = ident[0] * 2 + ident[1]
            gsend[t, d] = share(d)
            pltpu.make_async_remote_copy(
                src_ref=gsend.at[t, d], dst_ref=grecv.at[t, rho],
                send_sem=ssem.at[5 + t], recv_sem=rsem.at[5 + t],
                device_id=ident, device_id_type=MESH,
            ).start()
        grecv[t, rho] = share(rho)
        if t == 0:
            loglik_over_col(0)
            row = loglik_total(0) * advance
            valid = lax.broadcasted_iota(jnp.int32, (1, TP), 1) < K
            top = jnp.max(jnp.where(valid, row, -jnp.inf))
            clipped = jnp.maximum(row - top, -CLIP_FLOOR)
            norm = jnp.sum(jnp.where(valid, jnp.exp(clipped), 0.0))
            logw = clipped - jnp.log(norm)
            lw_ref[...] = logw[:, :K]
            weight = as_column(jnp.exp(logw))
            acc = jnp.zeros((1, TP), f32)
            for d in range(NR):
                cols = pl.ds(d * WR, WR)
                block = c[:, cols]
                center = jnp.sum(weight * block, axis=0, keepdims=True)
                wide = jnp.sum(weight * (block - center) ** 2, axis=0, keepdims=True) + 1e-06
                spread[:, cols] = wide
                for h in range(WR // TP):
                    acc = acc + wide[:, h * TP:(h + 1) * TP]
            sp_send[0] = acc
            sp_col[me] = acc
            to_col(sp_send.at[0], sp_col.at[me], None, ssem.at[9], rsem.at[9])

        landed(grecv.at[t, pl.ds(0, NR - 1)], rsem.at[5 + t])
        hfull[t, rho] = jnp.sum(grecv[t].astype(f32), axis=0).astype(bf16)
        to_row(hfull.at[t, rho], hfull.at[t, rho], ssem.at[7 + t], rsem.at[7 + t])

        if t == 0:
            landed(sp_col.at[pl.ds(0, NT - 1)], rsem.at[9])
            total = jnp.sum(jnp.sum(sp_col[...], axis=0))
            scale[...] = stepped * (spread[...] / (total / P_SIZE))
        for d in range(NR):
            cols = pl.ds(d * WR, WR)
            now = c[:, cols]
            a = scale[:, cols]
            pull = now / jnp.sqrt(now * now + 1.0)
            moved = now - (SHRINKAGE_LEVEL * a) * pull + jnp.sqrt(2.0 * a) * noise[t, :, cols]
            base[:, cols] = jnp.where(flags[t], moved, now)

        landed(hfull.at[t, pl.ds(0, NR - 1)], rsem.at[7 + t])
        for d in range(NR):
            cols = pl.ds(d * WR, WR)
            gain = jnp.where(flags[t], (upcoming * scale_s) * scale[:, cols], 0.0)
            fresh = base[:, cols] + gain * hfull[t, d].astype(f32)
            c[:, cols] = fresh
            cb[:, cols] = fresh.astype(bf16)
        if t == NMOVE - 1:
            pltpu.make_async_copy(c, out_hbm, osem).start()
        tile = logits_phase(t + 1, ps.at[t], rs.at[t], 1 + t)

    loglik_send(1, tile)
    loglik_over_col(1)
    ml_ref[...] = loglik_total(1)[:, :K] / float(ROWS * NR)

    pltpu.make_async_copy(c, out_hbm, osem).wait()
    landed(pf.at[pl.ds(0, NT - 1)], ssem.at[0])
    for t in range(NMOVE):
        landed(ps.at[t, pl.ds(0, NT - 1)], ssem.at[1 + t])
        landed(resid.at[t, pl.ds(0, NT - 1)], ssem.at[3 + t])
        landed(gsend.at[t, pl.ds(0, NR - 1)], ssem.at[5 + t])
        landed(hfull.at[t, pl.ds(0, NR - 1)], ssem.at[7 + t])
        landed(ll_col.at[t, pl.ds(0, NT - 1)], ssem.at[10 + t])
        landed(llr.at[t, pl.ds(0, NR - 1)], ssem.at[12 + t])
    landed(sp_col.at[pl.ds(0, NT - 1)], ssem.at[9])


def local(doses, status, cloud, noise, flags, heat, advance, drift):
    f32, bf16 = jnp.float32, jnp.bfloat16
    vmem = pl.BlockSpec(memory_space=pltpu.VMEM)
    smem = pl.BlockSpec(memory_space=pltpu.SMEM)
    hbm = pl.BlockSpec(memory_space=pl.ANY)
    particles, logw, mean = pl.pallas_call(
        kernel,
        out_shape=(
            jax.ShapeDtypeStruct((K, COLS), f32),
            jax.ShapeDtypeStruct((1, K), f32),
            jax.ShapeDtypeStruct((1, K), f32),
        ),
        in_specs=[hbm, vmem, hbm, hbm, vmem, smem, smem, smem],
        out_specs=(hbm, vmem, vmem),
        scratch_shapes=[
            pltpu.VMEM((NZ, TP, COLS), jnp.int32),
            pltpu.VMEM((ROWS, COLS), bf16),
            pltpu.VMEM((K, COLS), f32),
            pltpu.VMEM((NMOVE, K, COLS), f32),
            pltpu.VMEM((K, COLS), bf16),
            pltpu.VMEM((K, COLS), f32),
            pltpu.VMEM((1, COLS), f32),
            pltpu.VMEM((1, COLS), f32),
            pltpu.VMEM((K, ROWS), bf16),
            pltpu.VMEM((NT, TK, TP), f32),
            pltpu.VMEM((NT, TK, TP), f32),
            pltpu.VMEM((NMOVE, NT, TK, TP), bf16),
            pltpu.VMEM((NMOVE, NT, TK, TP), bf16),
            pltpu.VMEM((NMOVE, NT, TK, TP), bf16),
            pltpu.VMEM((NMOVE, NR, K, WR), bf16),
            pltpu.VMEM((NMOVE, NR, K, WR), bf16),
            pltpu.VMEM((NMOVE, NR, K, WR), bf16),
            pltpu.VMEM((2, 1, TP), f32),
            pltpu.VMEM((2, NT, 1, TP), f32),
            pltpu.VMEM((2, 1, TP), f32),
            pltpu.VMEM((2, NR, 1, TP), f32),
            pltpu.VMEM((1, 1, TP), f32),
            pltpu.VMEM((NT, 1, TP), f32),
            pltpu.SemaphoreType.DMA((NZ,)),
            pltpu.SemaphoreType.DMA((2,)),
            pltpu.SemaphoreType.DMA,
            pltpu.SemaphoreType.DMA((14,)),
            pltpu.SemaphoreType.DMA((14,)),
        ],
        compiler_params=pltpu.CompilerParams(collective_id=0, has_side_effects=True),
    )(doses, status.reshape(NZ, TP), cloud, noise, jnp.pad(flags, ((0, 0), (0, TP - K))), heat, advance, drift)
    return particles, logw.reshape(K), mean.reshape(K)


def solution(mesh):
    torus = Mesh(mesh.devices.reshape(4, 2, 8, 2, 2), ("row_0", "row_1", "col_0", "col_1", "col_2"))
    return jax.shard_map(
        local,
        mesh=torus,
        in_specs=(P(ROW, COL), P(ROW), P(None, COL), P(None, None, COL), P(), P(), P(), P()),
        out_specs=(P(None, COL), P(), P()),
        check_vma=False,
    )
```

```python
import jax
import jax.numpy as jnp
from jax import lax
from jax.experimental import pallas as pl
from jax.experimental.pallas import tpu as pltpu
from jax.sharding import Mesh
from jax.sharding import PartitionSpec as P

P_SIZE = 65536
K = 64
ROW = ("row_0", "row_1")
COL = ("col_0", "col_1", "col_2")
CLIP_FLOOR = 4.0
SHRINKAGE_LEVEL = 0.5
MESH = pl.DeviceIdType.MESH

ROWS = 1024
COLS = 2048
NZ, NQ, NT, NR = 8, 4, 32, 8
TP = 128
TK = 16
WR = COLS // NR
NMOVE = 2
Z_OFFSETS = (4, 3, 5, 2, 6, 1, 7, 0)
ROW_OFFSETS = ((2, 1), (1, 1), (3, 1), (2, 0), (0, 1), (1, 0), (3, 0))


def kernel(
    x_hbm, y_hbm, c_hbm, noise_hbm, flags_hbm, heat_hbm, adv_hbm, drift_hbm,
    out_hbm, lw_ref, ml_ref,
    xi, xb, c, noise, cb, base, spread, scale, y_ref, flags_ref, heat, adv, drift,
    pp, pq, pf, rf, ps, rs, resid, gsend, grecv, hfull,
    ll_send, ll_col, llr_send, llr, gm_send, gm_got, gm_all,
    xsem, lsem, osem, ssem, rsem, hsem, psem,
):
    f32, bf16 = jnp.float32, jnp.bfloat16
    y, xh = lax.axis_index("row_0"), lax.axis_index("row_1")
    z, xl, co = lax.axis_index("col_0"), lax.axis_index("col_1"), lax.axis_index("col_2")
    q = co * 2 + xl
    me = z * NQ + q
    rho = y * 2 + xh
    scale_s = float(P_SIZE) ** (-0.5)
    zs = [lax.rem(z + o, NZ) for o in Z_OFFSETS]
    peers = [(zd, qd, (y, xh, zd, qd % 2, qd // 2)) for zd in zs[:-1] for qd in range(NQ)]
    for o in range(1, NQ):
        qd = lax.rem(q + o, NQ)
        peers.append((z, qd, (y, xh, z, lax.rem(qd, 2), qd // 2)))
    row_peers = [(lax.rem(y + o[0], 4), lax.rem(xh + o[1], 2), z, xl, co) for o in ROW_OFFSETS]
    row_ids = [p[0] * 2 + p[1] for p in row_peers]
    row_from = [lax.rem(y + 4 - o[0], 4) * 2 + lax.rem(xh + o[1], 2) for o in ROW_OFFSETS]

    def send(src, dst, send_at, recv_at, device):
        pltpu.make_async_remote_copy(
            src_ref=src, dst_ref=dst, send_sem=send_at, recv_sem=recv_at,
            device_id=device, device_id_type=MESH,
        ).start()

    def landed(ref, sem):
        pltpu.make_async_copy(ref, ref, sem).wait()

    def people(zd):
        return pl.ds(pl.multiple_of(zd * TP, TP), TP)

    copy_c = pltpu.make_async_copy(c_hbm, c, lsem.at[0])
    copy_c.start()
    x_copies = [
        pltpu.make_async_copy(x_hbm.at[people(zd)], xi.at[k], xsem.at[k]) for k, zd in enumerate(zs)
    ]

    barrier = pltpu.get_barrier_semaphore()
    for _, _, device in peers:
        pl.semaphore_signal(barrier, inc=1, device_id=device, device_id_type=MESH)
    for device in row_peers:
        pl.semaphore_signal(barrier, inc=1, device_id=device, device_id_type=MESH)

    for copy in x_copies:
        copy.start()
    small = [
        pltpu.make_async_copy(src, dst, lsem.at[1 + i])
        for i, (src, dst) in enumerate((
            (y_hbm, y_ref), (flags_hbm, flags_ref), (heat_hbm, heat), (adv_hbm, adv),
            (drift_hbm, drift), (noise_hbm, noise),
        ))
    ]
    for copy in small:
        copy.start()

    def to_col(src, dst, send_at, recv_at):
        for _, _, device in peers:
            send(src, dst, send_at, recv_at, device)

    def to_row(src, dst, send_at, recv_at):
        for device in row_peers:
            send(src, dst, send_at, recv_at, device)

    def partial(zds):
        block = jnp.concatenate([xb[people(zd), :] for zd in zds], axis=0)
        return lax.dot_general(
            cb[...], block, (((1,), (1,)), ((), ())), preferred_element_type=f32
        )

    def collected(got, n, count):
        landed(got.at[pl.ds(0, count - 1)], rsem.at[n])
        return jnp.sum(got[...].astype(f32), axis=0) * scale_s

    def logits_phase(sent, got, n):
        groups = [(k, k + 1) for k in range(0, NZ, 2)]
        part = partial([zs[k] for k in groups[0]])
        for i, group in enumerate(groups):
            ahead = partial([zs[k] for k in groups[i + 1]]) if i + 1 < len(groups) else None
            for j, k in enumerate(group):
                for qd in range(NQ):
                    block = part[qd * TK:(qd + 1) * TK, j * TP:(j + 1) * TP]
                    sent[zs[k] * NQ + qd] = block.astype(sent.dtype)
                for zd, qd, device in peers[k * NQ:(k + 1) * NQ]:
                    send(sent.at[zd * NQ + qd], got.at[me], ssem.at[n], rsem.at[n], device)
            part = ahead
        got[me] = sent[me]
        return collected(got, n, NT)

    copy_c.wait()
    cb[...] = c[...].astype(bf16)
    half = NZ // 2
    for g in range(2):
        ks = range(g * half, (g + 1) * half)
        for k in ks:
            x_copies[k].wait()
            xb[people(zs[k]), :] = (xi[k].astype(f32) - 1.0).astype(bf16)
        part = partial([zs[k] for k in ks])
        for j, k in enumerate(ks):
            for h in range(2):
                pp[h, k] = part[h * 2 * TK:(h + 1) * 2 * TK, j * TP:(j + 1) * TP]
    pl.semaphore_wait(barrier, NT - 1 + NR - 1)

    other = (y, xh, z, xl, 1 - co)
    for g in range(2):
        ks = pl.ds(g * half, half)
        send(pp.at[1 - co, ks], pq.at[ks], ssem.at[0], psem.at[g], other)
    slot = z * 2 + xl
    for g in range(2):
        landed(pq.at[pl.ds(g * half, half)], psem.at[g])
        for k in range(g * half, (g + 1) * half):
            both = pp[co, k] + pq[k]
            for xd in range(2):
                pf[k, xd] = both[xd * TK:(xd + 1) * TK, :]
            if k < NZ - 1:
                for xd in range(2):
                    send(pf.at[k, xd], rf.at[slot], ssem.at[15], rsem.at[0], (y, xh, zs[k], xd, co))
            else:
                send(pf.at[k, 1 - xl], rf.at[slot], ssem.at[15], rsem.at[0], (y, xh, z, 1 - xl, co))
                rf[slot] = pf[k, xl]

    near = lax.broadcasted_iota(jnp.int32, (K // 2, TP), 1) < K
    gram = jnp.zeros((K, TP), f32)
    for d in range(NR):
        block = c[:, d * WR:(d + 1) * WR]
        block = block - jnp.mean(block, axis=0, keepdims=True)
        gram = gram + lax.dot_general(
            block, jnp.concatenate([block, block], axis=0), (((1,), (1,)), ((), ())),
            precision=lax.Precision.HIGHEST, preferred_element_type=f32,
        )
    folded = jnp.where(near, gram[:K // 2], gram[K // 2:])
    for d in range(NT):
        gm_send[d] = folded[d:d + 1, :]
    for zd, qd, device in peers:
        send(gm_send.at[zd * NQ + qd], gm_got.at[me], ssem.at[9], rsem.at[9], device)
    gm_got[me] = gm_send[me]

    for copy in small:
        copy.wait()
    outcome = y_ref[pl.ds(z, 1), :].astype(f32)
    sub = lax.broadcasted_iota(jnp.int32, (TK, TP), 0)
    lane = lax.broadcasted_iota(jnp.int32, (TK, TP), 1)

    def loglik_row(tile):
        soft = jnp.maximum(tile, 0.0) + jnp.log1p(jnp.exp(-jnp.abs(tile)))
        total = jnp.sum(outcome * tile - soft, axis=1, keepdims=True)
        return jnp.sum(jnp.where(lane == sub + q * TK, total, 0.0), axis=0, keepdims=True)

    eye = lax.broadcasted_iota(jnp.int32, (K, K), 0) == lax.broadcasted_iota(jnp.int32, (K, K), 1)

    def as_column(row):
        return jnp.sum(jnp.where(eye, row, 0.0), axis=1, keepdims=True)

    flags = [as_column(flags_ref[t:t + 1, :].astype(f32)) > 0.5 for t in range(NMOVE)]
    advance = adv[0]
    stepped = drift[0]
    upcoming = heat[0] + advance

    tile = collected(rf, 0, NT // 2)

    def loglik_send(u, tile):
        ll_send[u] = loglik_row(tile)
        ll_col[u, me] = ll_send[u]
        to_col(ll_send.at[u], ll_col.at[u, me], ssem.at[10 + u], rsem.at[10 + u])

    def loglik_over_col(u):
        landed(ll_col.at[u, pl.ds(0, NT - 1)], rsem.at[10 + u])
        llr_send[u] = jnp.sum(ll_col[u], axis=0)
        llr[u, rho] = llr_send[u]
        to_row(llr_send.at[u], llr.at[u, rho], ssem.at[12 + u], rsem.at[12 + u])

    def loglik_total(u):
        landed(llr.at[u, pl.ds(0, NR - 1)], rsem.at[12 + u])
        return jnp.sum(llr[u], axis=0)[:, :K]

    def free_part(t):
        for d in range(NR):
            cols = pl.ds(d * WR, WR)
            now = c[:, cols]
            a = scale[:, cols]
            pull = now / jnp.sqrt(now * now + 1.0)
            moved = now - (SHRINKAGE_LEVEL * a) * pull + jnp.sqrt(2.0 * a) * noise[t, :, cols]
            base[:, cols] = jnp.where(flags[t], moved, now)

    def update(t, d):
        cols = pl.ds(pl.multiple_of(d * WR, WR), WR)
        gain = jnp.where(flags[t], (upcoming * scale_s) * scale[:, cols], 0.0)
        fresh = base[:, cols] + gain * hfull[t, d].astype(f32)
        c[:, cols] = fresh
        cb[:, cols] = fresh.astype(bf16)

    for t in range(NMOVE):
        resid[t, me] = (outcome - jax.nn.sigmoid(tile)).astype(bf16)
        to_col(resid.at[t, me], resid.at[t, me], ssem.at[3 + t], rsem.at[3 + t])
        if t == 0:
            loglik_send(0, tile)
            landed(gm_got.at[pl.ds(0, NT - 1)], rsem.at[9])
            gm_all[me] = jnp.sum(gm_got[...], axis=0)
            to_col(gm_all.at[me], gm_all.at[me], ssem.at[14], rsem.at[14])
        landed(resid.at[t, pl.ds(0, NT - 1)], rsem.at[3 + t])
        if t == 0:
            loglik_over_col(0)

        whole = jnp.concatenate(
            [resid[t, p * NQ:(p + 1) * NQ].reshape(K, TP) for p in range(NZ)], axis=1
        )

        def shares(ds):
            block = jnp.concatenate(
                [xb[:, pl.ds(pl.multiple_of(d * WR, WR), WR)] for d in ds], axis=1
            )
            return jnp.dot(whole, block, preferred_element_type=f32).astype(bf16)

        order = row_ids + [rho]
        grad = shares(order[0:2])
        for g in range(0, NR, 2):
            ahead = shares(order[g + 2:g + 4]) if g + 2 < NR else None
            for j in range(2):
                i = g + j
                block = grad[:, j * WR:(j + 1) * WR]
                if i < NR - 1:
                    gsend[t, order[i]] = block
                    send(gsend.at[t, order[i]], grecv.at[t, rho], ssem.at[5 + t], rsem.at[5 + t], row_peers[i])
                else:
                    grecv[t, rho] = block
            grad = ahead
        if t > 0:
            free_part(t)

        landed(grecv.at[t, pl.ds(0, NR - 1)], rsem.at[5 + t])
        hfull[t, rho] = jnp.sum(grecv[t].astype(f32), axis=0).astype(bf16)
        for i, device in enumerate(row_peers):
            send(hfull.at[t, rho], hfull.at[t, rho], ssem.at[7 + t], hsem.at[t, i], device)

        if t == 0:
            row = loglik_total(0) * advance
            clipped = jnp.maximum(row - jnp.max(row), -CLIP_FLOOR)
            logw = clipped - jnp.log(jnp.sum(jnp.exp(clipped)))
            lw_ref[...] = logw
            weight = as_column(jnp.exp(logw))
            for d in range(NR):
                cols = pl.ds(d * WR, WR)
                block = c[:, cols]
                center = jnp.sum(weight * block, axis=0, keepdims=True)
                spread[:, cols] = jnp.sum(weight * (block - center) ** 2, axis=0, keepdims=True) + 1e-06
            landed(gm_all.at[pl.ds(0, NT - 1)], rsem.at[14])
            wide_sub = lax.broadcasted_iota(jnp.int32, (K, TP), 0)
            wide_lane = lax.rem(lax.broadcasted_iota(jnp.int32, (K, TP), 1), K)
            across = jnp.sum(jnp.where(wide_lane == wide_sub, weight, 0.0), axis=0, keepdims=True)
            term = weight * (jnp.where(wide_lane == wide_sub, 1.0, 0.0) - across)
            term = jnp.where(near, term[:K // 2], term[K // 2:])
            total = jnp.sum(term * gm_all[...].reshape(NT, TP)) + 1e-06 * P_SIZE
            scale[...] = stepped * (spread[...] / (total / P_SIZE))
            free_part(t)
        update(t, rho)
        for i in reversed(range(NR - 1)):
            landed(hfull.at[t, row_from[i]], hsem.at[t, i])
            update(t, row_from[i])
        if t == NMOVE - 1:
            pltpu.make_async_copy(c, out_hbm, osem).start()
        tile = logits_phase(ps.at[t], rs.at[t], 1 + t)

    loglik_send(1, tile)
    loglik_over_col(1)
    ml_ref[...] = loglik_total(1) / float(ROWS * NR)

    pltpu.make_async_copy(c, out_hbm, osem).wait()
    landed(pq, ssem.at[0])
    landed(rf.at[pl.ds(0, NT // 2 - 1)], ssem.at[15])
    for t in range(NMOVE):
        landed(ps.at[t, pl.ds(0, NT - 1)], ssem.at[1 + t])
        landed(resid.at[t, pl.ds(0, NT - 1)], ssem.at[3 + t])
        landed(gsend.at[t, pl.ds(0, NR - 1)], ssem.at[5 + t])
        landed(hfull.at[t, pl.ds(0, NR - 1)], ssem.at[7 + t])
        landed(ll_col.at[t, pl.ds(0, NT - 1)], ssem.at[10 + t])
        landed(llr.at[t, pl.ds(0, NR - 1)], ssem.at[12 + t])
    landed(gm_got.at[pl.ds(0, NT - 1)], ssem.at[9])
    landed(gm_all.at[pl.ds(0, NT - 1)], ssem.at[14])


def finish(c_in, lw_in, ml_in, c_out, lw_out, ml_out, buf, lw, ml, isem, osem):
    count = 4
    rows = K // count
    ins = [pltpu.make_async_copy(c_in.at[pl.ds(i * rows, rows)], buf.at[i], isem.at[i]) for i in range(count)]
    outs = [pltpu.make_async_copy(buf.at[i], c_out.at[pl.ds(i * rows, rows)], osem.at[i]) for i in range(count)]
    for src, via, dst in ((lw_in, lw, lw_out), (ml_in, ml, ml_out)):
        ins.append(pltpu.make_async_copy(src, via, isem.at[len(ins)]))
        outs.append(pltpu.make_async_copy(via, dst, osem.at[len(outs)]))
    for copy in ins:
        copy.start()
    for arrive, leave in zip(ins, outs):
        arrive.wait()
        leave.start()
    for copy in outs:
        copy.wait()


def local(doses, status, cloud, noise, flags, heat, advance, drift):
    f32, bf16 = jnp.float32, jnp.bfloat16
    vmem = pl.BlockSpec(memory_space=pltpu.VMEM)
    hbm = pl.BlockSpec(memory_space=pl.ANY)
    particles, logw, mean = pl.pallas_call(
        kernel,
        out_shape=(
            jax.ShapeDtypeStruct((K, COLS), f32),
            jax.ShapeDtypeStruct((1, K), f32),
            jax.ShapeDtypeStruct((1, K), f32),
        ),
        in_specs=[hbm] * 8,
        out_specs=(hbm, vmem, vmem),
        scratch_shapes=[
            pltpu.VMEM((NZ, TP, COLS), jnp.int32),
            pltpu.VMEM((ROWS, COLS), bf16),
            pltpu.VMEM((K, COLS), f32),
            pltpu.VMEM((NMOVE, K, COLS), f32),
            pltpu.VMEM((K, COLS), bf16),
            pltpu.VMEM((K, COLS), f32),
            pltpu.VMEM((1, COLS), f32),
            pltpu.VMEM((1, COLS), f32),
            pltpu.VMEM((NZ, TP), jnp.int32),
            pltpu.VMEM((NMOVE, K), jnp.int32),
            pltpu.SMEM((1,), f32),
            pltpu.SMEM((1,), f32),
            pltpu.SMEM((1,), f32),
            pltpu.VMEM((2, NZ, 2 * TK, TP), f32),
            pltpu.VMEM((NZ, 2 * TK, TP), f32),
            pltpu.VMEM((NZ, 2, TK, TP), f32),
            pltpu.VMEM((NT // 2, TK, TP), f32),
            pltpu.VMEM((NMOVE, NT, TK, TP), bf16),
            pltpu.VMEM((NMOVE, NT, TK, TP), bf16),
            pltpu.VMEM((NMOVE, NT, TK, TP), bf16),
            pltpu.VMEM((NMOVE, NR, K, WR), bf16),
            pltpu.VMEM((NMOVE, NR, K, WR), bf16),
            pltpu.VMEM((NMOVE, NR, K, WR), bf16),
            pltpu.VMEM((2, 1, TP), f32),
            pltpu.VMEM((2, NT, 1, TP), f32),
            pltpu.VMEM((2, 1, TP), f32),
            pltpu.VMEM((2, NR, 1, TP), f32),
            pltpu.VMEM((NT, 1, TP), f32),
            pltpu.VMEM((NT, 1, TP), f32),
            pltpu.VMEM((NT, 1, TP), f32),
            pltpu.SemaphoreType.DMA((NZ,)),
            pltpu.SemaphoreType.DMA((7,)),
            pltpu.SemaphoreType.DMA,
            pltpu.SemaphoreType.DMA((16,)),
            pltpu.SemaphoreType.DMA((15,)),
            pltpu.SemaphoreType.DMA((NMOVE, NR - 1)),
            pltpu.SemaphoreType.DMA((2,)),
        ],
        compiler_params=pltpu.CompilerParams(collective_id=0, has_side_effects=True),
    )(doses, status.reshape(NZ, TP), cloud, noise, flags, heat, advance, drift)
    particles, logw, mean = pl.pallas_call(
        finish,
        out_shape=(
            jax.ShapeDtypeStruct((K, COLS), f32),
            jax.ShapeDtypeStruct((1, K), f32),
            jax.ShapeDtypeStruct((1, K), f32),
        ),
        in_specs=[hbm] * 3,
        out_specs=(hbm, hbm, hbm),
        scratch_shapes=[
            pltpu.VMEM((4, K // 4, COLS), f32),
            pltpu.VMEM((1, K), f32),
            pltpu.VMEM((1, K), f32),
            pltpu.SemaphoreType.DMA((6,)),
            pltpu.SemaphoreType.DMA((6,)),
        ],
    )(particles, logw, mean)
    return particles, logw.reshape(K), mean.reshape(K)


def solution(mesh):
    torus = Mesh(mesh.devices.reshape(4, 2, 8, 2, 2), ("row_0", "row_1", "col_0", "col_1", "col_2"))
    return jax.shard_map(
        local,
        mesh=torus,
        in_specs=(P(ROW, COL), P(ROW), P(None, COL), P(None, None, COL), P(), P(), P(), P()),
        out_specs=(P(None, COL), P(), P()),
        check_vma=False,
    )
```

```python
import jax
import jax.numpy as jnp
from jax import lax
from jax.experimental import pallas as pl
from jax.experimental.pallas import tpu as pltpu
from jax.sharding import Mesh
from jax.sharding import PartitionSpec as P

P_SIZE = 65536
K = 64
ROW = ("row_0", "row_1")
COL = ("col_0", "col_1", "col_2")
CLIP_FLOOR = 4.0
SHRINKAGE_LEVEL = 0.5
MESH = pl.DeviceIdType.MESH

ROWS = 1024
COLS = 2048
NZ, NQ, NT, NR = 8, 4, 32, 8
TP = 128
TK = 16
WR = COLS // NR
NMOVE = 2
AHEAD = 4
Z_OFFSETS = (4, 3, 5, 2, 6, 1, 7, 0)
ROW_OFFSETS = ((2, 1), (1, 1), (3, 1), (2, 0), (0, 1), (1, 0), (3, 0))


def kernel(
    x_hbm, y_hbm, c_hbm, noise_hbm, flags_hbm, heat_hbm, adv_hbm, drift_hbm,
    c, lw_ref, ml_ref,
    xi, xb, noise, cb, base, spread, scale, y_ref, flags_ref, heat, adv, drift,
    pp, pq, pf, rf, ps, rs, resid, gsend, grecv, hfull,
    ll_send, ll_col, llr_send, llr, gm_send, gm_got, gm_all,
    xsem, lsem, ssem, rsem, hsem, psem,
):
    f32, bf16 = jnp.float32, jnp.bfloat16
    y, xh = lax.axis_index("row_0"), lax.axis_index("row_1")
    z, xl, co = lax.axis_index("col_0"), lax.axis_index("col_1"), lax.axis_index("col_2")
    q = co * 2 + xl
    me = z * NQ + q
    rho = y * 2 + xh
    scale_s = float(P_SIZE) ** (-0.5)
    zs = [lax.rem(z + o, NZ) for o in Z_OFFSETS]
    peers = [(zd, qd, (y, xh, zd, qd % 2, qd // 2)) for zd in zs[:-1] for qd in range(NQ)]
    for o in range(1, NQ):
        qd = lax.rem(q + o, NQ)
        peers.append((z, qd, (y, xh, z, lax.rem(qd, 2), qd // 2)))
    row_peers = [(lax.rem(y + o[0], 4), lax.rem(xh + o[1], 2), z, xl, co) for o in ROW_OFFSETS]
    row_ids = [p[0] * 2 + p[1] for p in row_peers]
    row_from = [lax.rem(y + 4 - o[0], 4) * 2 + lax.rem(xh + o[1], 2) for o in ROW_OFFSETS]

    def send(src, dst, send_at, recv_at, device):
        pltpu.make_async_remote_copy(
            src_ref=src, dst_ref=dst, send_sem=send_at, recv_sem=recv_at,
            device_id=device, device_id_type=MESH,
        ).start()

    def landed(ref, sem):
        pltpu.make_async_copy(ref, ref, sem).wait()

    def people(zd):
        return pl.ds(pl.multiple_of(zd * TP, TP), TP)

    copy_c = pltpu.make_async_copy(c_hbm, c, lsem.at[0])
    copy_c.start()
    x_copies = [
        pltpu.make_async_copy(x_hbm.at[people(zd)], xi.at[k], xsem.at[k]) for k, zd in enumerate(zs)
    ]

    for copy in x_copies[:AHEAD]:
        copy.start()

    barrier = pltpu.get_barrier_semaphore()
    for _, _, device in peers:
        pl.semaphore_signal(barrier, inc=1, device_id=device, device_id_type=MESH)
    for device in row_peers:
        pl.semaphore_signal(barrier, inc=1, device_id=device, device_id_type=MESH)

    small = [
        pltpu.make_async_copy(src, dst, lsem.at[1 + i])
        for i, (src, dst) in enumerate((
            (y_hbm, y_ref), (flags_hbm, flags_ref), (heat_hbm, heat), (adv_hbm, adv),
            (drift_hbm, drift), (noise_hbm, noise),
        ))
    ]

    def to_col(src, dst, send_at, recv_at):
        for _, _, device in peers:
            send(src, dst, send_at, recv_at, device)

    def to_row(src, dst, send_at, recv_at):
        for device in row_peers:
            send(src, dst, send_at, recv_at, device)

    def partial(zds):
        block = jnp.concatenate([xb[people(zd), :] for zd in zds], axis=0)
        return lax.dot_general(
            cb[...], block, (((1,), (1,)), ((), ())), preferred_element_type=f32
        )

    def collected(got, n, count):
        landed(got.at[pl.ds(0, count - 1)], rsem.at[n])
        return jnp.sum(got[...].astype(f32), axis=0) * scale_s

    def logits_phase(sent, got, n):
        groups = [(k, k + 1) for k in range(0, NZ, 2)]
        part = partial([zs[k] for k in groups[0]])
        for i, group in enumerate(groups):
            ahead = partial([zs[k] for k in groups[i + 1]]) if i + 1 < len(groups) else None
            for j, k in enumerate(group):
                for qd in range(NQ):
                    block = part[qd * TK:(qd + 1) * TK, j * TP:(j + 1) * TP]
                    sent[zs[k] * NQ + qd] = block.astype(sent.dtype)
                for zd, qd, device in peers[k * NQ:(k + 1) * NQ]:
                    send(sent.at[zd * NQ + qd], got.at[me], ssem.at[n], rsem.at[n], device)
            part = ahead
        got[me] = sent[me]
        return collected(got, n, NT)

    def arrive(g):
        for k in (g, g + 1):
            x_copies[k].wait()
            if k + AHEAD < NZ:
                x_copies[k + AHEAD].start()

    def convert(g):
        for k in (g, g + 1):
            xb[people(zs[k]), :] = (xi[k].astype(f32) - 1.0).astype(bf16)

    def keep(g, part):
        for j in range(2):
            for h in range(2):
                pp[h, g + j] = part[h * 2 * TK:(h + 1) * 2 * TK, j * TP:(j + 1) * TP]

    half = NZ // 2
    other = (y, xh, z, xl, 1 - co)
    slot = z * 2 + xl

    def swap(g):
        ks = pl.ds(g * half, half)
        send(pp.at[1 - co, ks], pq.at[ks], ssem.at[0], psem.at[g], other)

    def joined(g):
        landed(pq.at[pl.ds(g * half, half)], psem.at[g])
        for k in range(g * half, (g + 1) * half):
            both = pp[co, k] + pq[k]
            for xd in range(2):
                pf[k, xd] = both[xd * TK:(xd + 1) * TK, :]
            if k < NZ - 1:
                for xd in range(2):
                    send(pf.at[k, xd], rf.at[slot], ssem.at[15], rsem.at[0], (y, xh, zs[k], xd, co))
            else:
                send(pf.at[k, 1 - xl], rf.at[slot], ssem.at[15], rsem.at[0], (y, xh, z, 1 - xl, co))
                rf[slot] = pf[k, xl]

    arrive(0)
    convert(0)
    copy_c.wait()
    cb[...] = c[...].astype(bf16)
    part = partial(zs[0:2])
    arrive(2)
    convert(2)
    keep(0, part)
    part = partial(zs[2:4])
    arrive(4)
    convert(4)
    keep(2, part)
    pl.semaphore_wait(barrier, NT - 1 + NR - 1)
    swap(0)
    part = partial(zs[4:6])
    arrive(6)
    convert(6)
    keep(4, part)
    joined(0)
    part = partial(zs[6:8])
    keep(6, part)
    swap(1)
    for copy in small:
        copy.start()
    joined(1)

    near = lax.broadcasted_iota(jnp.int32, (K // 2, TP), 1) < K
    gram = jnp.zeros((K, TP), f32)
    for d in range(NR):
        block = c[:, d * WR:(d + 1) * WR]
        block = block - jnp.mean(block, axis=0, keepdims=True)
        gram = gram + lax.dot_general(
            block, jnp.concatenate([block, block], axis=0), (((1,), (1,)), ((), ())),
            precision=lax.Precision.HIGHEST, preferred_element_type=f32,
        )
    folded = jnp.where(near, gram[:K // 2], gram[K // 2:])
    for d in range(NT):
        gm_send[d] = folded[d:d + 1, :]
    for zd, qd, device in peers:
        send(gm_send.at[zd * NQ + qd], gm_got.at[me], ssem.at[9], rsem.at[9], device)
    gm_got[me] = gm_send[me]

    for copy in small:
        copy.wait()
    outcome = y_ref[pl.ds(z, 1), :].astype(f32)
    sub = lax.broadcasted_iota(jnp.int32, (TK, TP), 0)
    lane = lax.broadcasted_iota(jnp.int32, (TK, TP), 1)

    def loglik_row(tile):
        soft = jnp.maximum(tile, 0.0) + jnp.log1p(jnp.exp(-jnp.abs(tile)))
        total = jnp.sum(outcome * tile - soft, axis=1, keepdims=True)
        return jnp.sum(jnp.where(lane == sub + q * TK, total, 0.0), axis=0, keepdims=True)

    eye = lax.broadcasted_iota(jnp.int32, (K, K), 0) == lax.broadcasted_iota(jnp.int32, (K, K), 1)

    def as_column(row):
        return jnp.sum(jnp.where(eye, row, 0.0), axis=1, keepdims=True)

    flags = [as_column(flags_ref[t:t + 1, :].astype(f32)) > 0.5 for t in range(NMOVE)]
    advance = adv[0]
    stepped = drift[0]
    upcoming = heat[0] + advance

    tile = collected(rf, 0, NT // 2)

    def loglik_send(u, tile):
        ll_send[u] = loglik_row(tile)
        ll_col[u, me] = ll_send[u]
        to_col(ll_send.at[u], ll_col.at[u, me], ssem.at[10 + u], rsem.at[10 + u])

    def loglik_over_col(u):
        landed(ll_col.at[u, pl.ds(0, NT - 1)], rsem.at[10 + u])
        llr_send[u] = jnp.sum(ll_col[u], axis=0)
        llr[u, rho] = llr_send[u]
        to_row(llr_send.at[u], llr.at[u, rho], ssem.at[12 + u], rsem.at[12 + u])

    def loglik_total(u):
        landed(llr.at[u, pl.ds(0, NR - 1)], rsem.at[12 + u])
        return jnp.sum(llr[u], axis=0)[:, :K]

    def free_part(t):
        for d in range(NR):
            cols = pl.ds(d * WR, WR)
            now = c[:, cols]
            a = scale[:, cols]
            pull = now / jnp.sqrt(now * now + 1.0)
            moved = now - (SHRINKAGE_LEVEL * a) * pull + jnp.sqrt(2.0 * a) * noise[t, :, cols]
            base[:, cols] = jnp.where(flags[t], moved, now)

    def update(t, d):
        cols = pl.ds(pl.multiple_of(d * WR, WR), WR)
        gain = jnp.where(flags[t], (upcoming * scale_s) * scale[:, cols], 0.0)
        fresh = base[:, cols] + gain * hfull[t, d].astype(f32)
        c[:, cols] = fresh
        cb[:, cols] = fresh.astype(bf16)

    for t in range(NMOVE):
        resid[t, me] = (outcome - jax.nn.sigmoid(tile)).astype(bf16)
        to_col(resid.at[t, me], resid.at[t, me], ssem.at[3 + t], rsem.at[3 + t])
        if t == 0:
            loglik_send(0, tile)
        landed(resid.at[t, pl.ds(0, NT - 1)], rsem.at[3 + t])

        whole = jnp.concatenate(
            [resid[t, p * NQ:(p + 1) * NQ].reshape(K, TP) for p in range(NZ)], axis=1
        )

        def shares(ds):
            block = jnp.concatenate(
                [xb[:, pl.ds(pl.multiple_of(d * WR, WR), WR)] for d in ds], axis=1
            )
            return jnp.dot(whole, block, preferred_element_type=f32).astype(bf16)

        order = row_ids + [rho]
        grad = shares(order[0:2])
        for g in range(0, NR, 2):
            ahead = shares(order[g + 2:g + 4]) if g + 2 < NR else None
            for j in range(2):
                i = g + j
                block = grad[:, j * WR:(j + 1) * WR]
                if i < NR - 1:
                    gsend[t, order[i]] = block
                    send(gsend.at[t, order[i]], grecv.at[t, rho], ssem.at[5 + t], rsem.at[5 + t], row_peers[i])
                else:
                    grecv[t, rho] = block
            grad = ahead
            if t == 0 and g == 0:
                loglik_over_col(0)
        if t == 0:
            landed(gm_got.at[pl.ds(0, NT - 1)], rsem.at[9])
            gm_all[me] = jnp.sum(gm_got[...], axis=0)
            to_col(gm_all.at[me], gm_all.at[me], ssem.at[14], rsem.at[14])
        else:
            free_part(t)

        landed(grecv.at[t, pl.ds(0, NR - 1)], rsem.at[5 + t])
        hfull[t, rho] = jnp.sum(grecv[t].astype(f32), axis=0).astype(bf16)
        for i, device in enumerate(row_peers):
            send(hfull.at[t, rho], hfull.at[t, rho], ssem.at[7 + t], hsem.at[t, i], device)

        if t == 0:
            row = loglik_total(0) * advance
            clipped = jnp.maximum(row - jnp.max(row), -CLIP_FLOOR)
            logw = clipped - jnp.log(jnp.sum(jnp.exp(clipped)))
            lw_ref[...] = logw
            weight = as_column(jnp.exp(logw))
            for d in range(NR):
                cols = pl.ds(d * WR, WR)
                block = c[:, cols]
                center = jnp.sum(weight * block, axis=0, keepdims=True)
                spread[:, cols] = jnp.sum(weight * (block - center) ** 2, axis=0, keepdims=True) + 1e-06
            landed(gm_all.at[pl.ds(0, NT - 1)], rsem.at[14])
            wide_sub = lax.broadcasted_iota(jnp.int32, (K, TP), 0)
            wide_lane = lax.rem(lax.broadcasted_iota(jnp.int32, (K, TP), 1), K)
            across = jnp.sum(jnp.where(wide_lane == wide_sub, weight, 0.0), axis=0, keepdims=True)
            term = weight * (jnp.where(wide_lane == wide_sub, 1.0, 0.0) - across)
            term = jnp.where(near, term[:K // 2], term[K // 2:])
            total = jnp.sum(term * gm_all[...].reshape(NT, TP)) + 1e-06 * P_SIZE
            scale[...] = stepped * (spread[...] / (total / P_SIZE))
            free_part(t)
        update(t, rho)
        for i in reversed(range(NR - 1)):
            landed(hfull.at[t, row_from[i]], hsem.at[t, i])
            update(t, row_from[i])
        tile = logits_phase(ps.at[t], rs.at[t], 1 + t)

    loglik_send(1, tile)
    loglik_over_col(1)
    ml_ref[...] = loglik_total(1) / float(ROWS * NR)

    landed(pq, ssem.at[0])
    landed(rf.at[pl.ds(0, NT // 2 - 1)], ssem.at[15])
    for t in range(NMOVE):
        landed(ps.at[t, pl.ds(0, NT - 1)], ssem.at[1 + t])
        landed(resid.at[t, pl.ds(0, NT - 1)], ssem.at[3 + t])
        landed(gsend.at[t, pl.ds(0, NR - 1)], ssem.at[5 + t])
        landed(hfull.at[t, pl.ds(0, NR - 1)], ssem.at[7 + t])
        landed(ll_col.at[t, pl.ds(0, NT - 1)], ssem.at[10 + t])
        landed(llr.at[t, pl.ds(0, NR - 1)], ssem.at[12 + t])
    landed(gm_got.at[pl.ds(0, NT - 1)], ssem.at[9])
    landed(gm_all.at[pl.ds(0, NT - 1)], ssem.at[14])


def finish(c_in, lw_in, ml_in, c_out, lw_out, ml_out, sem):
    copies = [
        pltpu.make_async_copy(src, dst, sem.at[i])
        for i, (src, dst) in enumerate(((ml_in, ml_out), (lw_in, lw_out), (c_in, c_out)))
    ]
    for copy in copies:
        copy.start()
    for copy in copies:
        copy.wait()


def local(doses, status, cloud, noise, flags, heat, advance, drift):
    f32, bf16 = jnp.float32, jnp.bfloat16
    vmem = pl.BlockSpec(memory_space=pltpu.VMEM)
    hbm = pl.BlockSpec(memory_space=pl.ANY)
    particles, logw, mean = pl.pallas_call(
        kernel,
        out_shape=(
            pltpu.VMEM((K, COLS), f32),
            pltpu.VMEM((1, K), f32),
            pltpu.VMEM((1, K), f32),
        ),
        in_specs=[hbm] * 8,
        out_specs=(vmem, vmem, vmem),
        scratch_shapes=[
            pltpu.VMEM((NZ, TP, COLS), jnp.int32),
            pltpu.VMEM((ROWS, COLS), bf16),
            pltpu.VMEM((NMOVE, K, COLS), f32),
            pltpu.VMEM((K, COLS), bf16),
            pltpu.VMEM((K, COLS), f32),
            pltpu.VMEM((1, COLS), f32),
            pltpu.VMEM((1, COLS), f32),
            pltpu.VMEM((NZ, TP), jnp.int32),
            pltpu.VMEM((NMOVE, K), jnp.int32),
            pltpu.SMEM((1,), f32),
            pltpu.SMEM((1,), f32),
            pltpu.SMEM((1,), f32),
            pltpu.VMEM((2, NZ, 2 * TK, TP), f32),
            pltpu.VMEM((NZ, 2 * TK, TP), f32),
            pltpu.VMEM((NZ, 2, TK, TP), f32),
            pltpu.VMEM((NT // 2, TK, TP), f32),
            pltpu.VMEM((NMOVE, NT, TK, TP), bf16),
            pltpu.VMEM((NMOVE, NT, TK, TP), bf16),
            pltpu.VMEM((NMOVE, NT, TK, TP), bf16),
            pltpu.VMEM((NMOVE, NR, K, WR), bf16),
            pltpu.VMEM((NMOVE, NR, K, WR), bf16),
            pltpu.VMEM((NMOVE, NR, K, WR), bf16),
            pltpu.VMEM((2, 1, TP), f32),
            pltpu.VMEM((2, NT, 1, TP), f32),
            pltpu.VMEM((2, 1, TP), f32),
            pltpu.VMEM((2, NR, 1, TP), f32),
            pltpu.VMEM((NT, 1, TP), f32),
            pltpu.VMEM((NT, 1, TP), f32),
            pltpu.VMEM((NT, 1, TP), f32),
            pltpu.SemaphoreType.DMA((NZ,)),
            pltpu.SemaphoreType.DMA((7,)),
            pltpu.SemaphoreType.DMA((16,)),
            pltpu.SemaphoreType.DMA((15,)),
            pltpu.SemaphoreType.DMA((NMOVE, NR - 1)),
            pltpu.SemaphoreType.DMA((2,)),
        ],
        compiler_params=pltpu.CompilerParams(collective_id=0, has_side_effects=True),
    )(doses, status.reshape(NZ, TP), cloud, noise, flags, heat, advance, drift)
    particles, logw, mean = pl.pallas_call(
        finish,
        out_shape=(
            jax.ShapeDtypeStruct((K, COLS), f32),
            jax.ShapeDtypeStruct((1, K), f32),
            jax.ShapeDtypeStruct((1, K), f32),
        ),
        in_specs=[vmem] * 3,
        out_specs=(hbm, hbm, hbm),
        scratch_shapes=[pltpu.SemaphoreType.DMA((3,))],
        compiler_params=pltpu.CompilerParams(vmem_limit_bytes=1 << 20),
    )(particles, logw, mean)
    return particles, logw.reshape(K), mean.reshape(K)


def solution(mesh):
    torus = Mesh(mesh.devices.reshape(4, 2, 8, 2, 2), ("row_0", "row_1", "col_0", "col_1", "col_2"))
    return jax.shard_map(
        local,
        mesh=torus,
        in_specs=(P(ROW, COL), P(ROW), P(None, COL), P(None, None, COL), P(), P(), P(), P()),
        out_specs=(P(None, COL), P(), P()),
        check_vma=False,
    )
```

```python
import jax
import jax.numpy as jnp
from jax import lax
from jax.experimental import pallas as pl
from jax.experimental.pallas import tpu as pltpu
from jax.sharding import Mesh
from jax.sharding import PartitionSpec as P

P_SIZE = 65536
K = 64
ROW = ("row_0", "row_1")
COL = ("col_0", "col_1", "col_2")
CLIP_FLOOR = 4.0
SHRINKAGE_LEVEL = 0.5
MESH = pl.DeviceIdType.MESH

ROWS = 1024
COLS = 2048
NZ, NQ, NT, NR = 8, 4, 32, 8
TP = 128
TK = 16
WR = COLS // NR
NMOVE = 2
NALL = 128
ALL_OFFSETS = sorted(
    ((a, b, c, d) for a in range(4) for b in range(2) for c in range(8) for d in range(2) if a + b + c + d),
    key=lambda o: -(min(o[0], 4 - o[0]) + min(o[2], 8 - o[2]) + (0, 1, 2, 1)[2 * o[1] + o[3]]),
)
AHEAD = 4
Z_OFFSETS = (4, 3, 5, 2, 6, 1, 7, 0)
ROW_OFFSETS = ((2, 1), (1, 1), (3, 1), (2, 0), (0, 1), (1, 0), (3, 0))


def kernel(
    x_hbm, y_hbm, c_hbm, noise_hbm, flags_hbm, heat_hbm, adv_hbm, drift_hbm,
    c, lw_ref, ml_ref,
    xi, xb, noise, cb, base, spread, scale, y_ref, flags_ref, heat, adv, drift,
    pp, pq, pf, rf, ps, rs, resid, gsend, grecv, hfull,
    fin_pair, fin_send, fin_all, ll_send, ll_col, llr_send, llr, gm_send, gm_got, gm_all,
    xsem, lsem, ssem, rsem, hsem, psem,
):
    f32, bf16 = jnp.float32, jnp.bfloat16
    y, xh = lax.axis_index("row_0"), lax.axis_index("row_1")
    z, xl, co = lax.axis_index("col_0"), lax.axis_index("col_1"), lax.axis_index("col_2")
    q = co * 2 + xl
    me = z * NQ + q
    rho = y * 2 + xh
    scale_s = float(P_SIZE) ** (-0.5)
    zs = [lax.rem(z + o, NZ) for o in Z_OFFSETS]
    peers = [(zd, qd, (y, xh, zd, qd % 2, qd // 2)) for zd in zs[:-1] for qd in range(NQ)]
    for o in range(1, NQ):
        qd = lax.rem(q + o, NQ)
        peers.append((z, qd, (y, xh, z, lax.rem(qd, 2), qd // 2)))
    row_peers = [(lax.rem(y + o[0], 4), lax.rem(xh + o[1], 2), z, xl, co) for o in ROW_OFFSETS]
    row_ids = [p[0] * 2 + p[1] for p in row_peers]
    row_from = [lax.rem(y + 4 - o[0], 4) * 2 + lax.rem(xh + o[1], 2) for o in ROW_OFFSETS]

    def send(src, dst, send_at, recv_at, device):
        pltpu.make_async_remote_copy(
            src_ref=src, dst_ref=dst, send_sem=send_at, recv_sem=recv_at,
            device_id=device, device_id_type=MESH,
        ).start()

    def landed(ref, sem):
        pltpu.make_async_copy(ref, ref, sem).wait()

    def people(zd):
        return pl.ds(pl.multiple_of(zd * TP, TP), TP)

    copy_c = pltpu.make_async_copy(c_hbm, c, lsem.at[0])
    copy_c.start()
    x_copies = [
        pltpu.make_async_copy(x_hbm.at[people(zd)], xi.at[k], xsem.at[k]) for k, zd in enumerate(zs)
    ]

    for copy in x_copies[:AHEAD]:
        copy.start()

    barrier = pltpu.get_barrier_semaphore()
    for _, _, device in peers:
        pl.semaphore_signal(barrier, inc=1, device_id=device, device_id_type=MESH)
    for device in row_peers:
        pl.semaphore_signal(barrier, inc=1, device_id=device, device_id_type=MESH)

    small = [
        pltpu.make_async_copy(src, dst, lsem.at[1 + i])
        for i, (src, dst) in enumerate((
            (y_hbm, y_ref), (flags_hbm, flags_ref), (heat_hbm, heat), (adv_hbm, adv),
            (drift_hbm, drift), (noise_hbm, noise),
        ))
    ]

    def to_col(src, dst, send_at, recv_at):
        for _, _, device in peers:
            send(src, dst, send_at, recv_at, device)

    def to_row(src, dst, send_at, recv_at):
        for device in row_peers:
            send(src, dst, send_at, recv_at, device)

    def partial(zds):
        block = jnp.concatenate([xb[people(zd), :] for zd in zds], axis=0)
        return lax.dot_general(
            cb[...], block, (((1,), (1,)), ((), ())), preferred_element_type=f32
        )

    def collected(got, n, count):
        landed(got.at[pl.ds(0, count - 1)], rsem.at[n])
        return jnp.sum(got[...].astype(f32), axis=0) * scale_s

    def logits_phase(sent, got, n):
        groups = [(k, k + 1) for k in range(0, NZ, 2)]
        part = partial([zs[k] for k in groups[0]])
        for i, group in enumerate(groups):
            ahead = partial([zs[k] for k in groups[i + 1]]) if i + 1 < len(groups) else None
            for j, k in enumerate(group):
                for qd in range(NQ):
                    block = part[qd * TK:(qd + 1) * TK, j * TP:(j + 1) * TP]
                    sent[zs[k] * NQ + qd] = block.astype(sent.dtype)
                for zd, qd, device in peers[k * NQ:(k + 1) * NQ]:
                    send(sent.at[zd * NQ + qd], got.at[me], ssem.at[n], rsem.at[n], device)
            part = ahead
        got[me] = sent[me]
        return collected(got, n, NT)

    def arrive(g):
        for k in (g, g + 1):
            x_copies[k].wait()
            if k + AHEAD < NZ:
                x_copies[k + AHEAD].start()

    def convert(g):
        for k in (g, g + 1):
            xb[people(zs[k]), :] = (xi[k].astype(f32) - 1.0).astype(bf16)

    def keep(g, part):
        for j in range(2):
            for h in range(2):
                pp[h, g + j] = part[h * 2 * TK:(h + 1) * 2 * TK, j * TP:(j + 1) * TP]

    half = NZ // 2
    other = (y, xh, z, xl, 1 - co)
    slot = z * 2 + xl

    def swap(g):
        ks = pl.ds(g * half, half)
        send(pp.at[1 - co, ks], pq.at[ks], ssem.at[0], psem.at[g], other)

    def joined(g):
        landed(pq.at[pl.ds(g * half, half)], psem.at[g])
        for k in range(g * half, (g + 1) * half):
            both = pp[co, k] + pq[k]
            for xd in range(2):
                pf[k, xd] = both[xd * TK:(xd + 1) * TK, :]
            if k < NZ - 1:
                for xd in range(2):
                    send(pf.at[k, xd], rf.at[slot], ssem.at[15], rsem.at[0], (y, xh, zs[k], xd, co))
            else:
                send(pf.at[k, 1 - xl], rf.at[slot], ssem.at[15], rsem.at[0], (y, xh, z, 1 - xl, co))
                rf[slot] = pf[k, xl]

    arrive(0)
    convert(0)
    copy_c.wait()
    cb[...] = c[...].astype(bf16)
    part = partial(zs[0:2])
    arrive(2)
    convert(2)
    keep(0, part)
    part = partial(zs[2:4])
    arrive(4)
    convert(4)
    keep(2, part)
    pl.semaphore_wait(barrier, NT - 1 + NR - 1)
    swap(0)
    part = partial(zs[4:6])
    arrive(6)
    convert(6)
    keep(4, part)
    joined(0)
    part = partial(zs[6:8])
    keep(6, part)
    swap(1)
    for copy in small:
        copy.start()
    joined(1)

    near = lax.broadcasted_iota(jnp.int32, (K // 2, TP), 1) < K
    gram = jnp.zeros((K, TP), f32)
    for d in range(NR):
        block = c[:, d * WR:(d + 1) * WR]
        block = block - jnp.mean(block, axis=0, keepdims=True)
        gram = gram + lax.dot_general(
            block, jnp.concatenate([block, block], axis=0), (((1,), (1,)), ((), ())),
            precision=lax.Precision.HIGHEST, preferred_element_type=f32,
        )
    folded = jnp.where(near, gram[:K // 2], gram[K // 2:])
    for d in range(NT):
        gm_send[d] = folded[d:d + 1, :]
    for zd, qd, device in peers:
        send(gm_send.at[zd * NQ + qd], gm_got.at[me], ssem.at[9], rsem.at[9], device)
    gm_got[me] = gm_send[me]

    for copy in small:
        copy.wait()
    outcome = y_ref[pl.ds(z, 1), :].astype(f32)
    sub = lax.broadcasted_iota(jnp.int32, (TK, TP), 0)
    lane = lax.broadcasted_iota(jnp.int32, (TK, TP), 1)

    def loglik_row(tile):
        soft = jnp.maximum(tile, 0.0) + jnp.log1p(jnp.exp(-jnp.abs(tile)))
        total = jnp.sum(outcome * tile - soft, axis=1, keepdims=True)
        return jnp.sum(jnp.where(lane == sub + q * TK, total, 0.0), axis=0, keepdims=True)

    eye = lax.broadcasted_iota(jnp.int32, (K, K), 0) == lax.broadcasted_iota(jnp.int32, (K, K), 1)

    def as_column(row):
        return jnp.sum(jnp.where(eye, row, 0.0), axis=1, keepdims=True)

    flags = [as_column(flags_ref[t:t + 1, :].astype(f32)) > 0.5 for t in range(NMOVE)]
    advance = adv[0]
    stepped = drift[0]
    upcoming = heat[0] + advance

    tile = collected(rf, 0, NT // 2)

    def loglik_send(u, tile):
        ll_send[u] = loglik_row(tile)
        ll_col[u, me] = ll_send[u]
        to_col(ll_send.at[u], ll_col.at[u, me], ssem.at[10 + u], rsem.at[10 + u])

    def loglik_over_col(u):
        landed(ll_col.at[u, pl.ds(0, NT - 1)], rsem.at[10 + u])
        llr_send[u] = jnp.sum(ll_col[u], axis=0)
        llr[u, rho] = llr_send[u]
        to_row(llr_send.at[u], llr.at[u, rho], ssem.at[12 + u], rsem.at[12 + u])

    def loglik_total(u):
        landed(llr.at[u, pl.ds(0, NR - 1)], rsem.at[12 + u])
        return jnp.sum(llr[u], axis=0)[:, :K]

    def free_part(t):
        for d in range(NR):
            cols = pl.ds(d * WR, WR)
            now = c[:, cols]
            a = scale[:, cols]
            pull = now / jnp.sqrt(now * now + 1.0)
            moved = now - (SHRINKAGE_LEVEL * a) * pull + jnp.sqrt(2.0 * a) * noise[t, :, cols]
            base[:, cols] = jnp.where(flags[t], moved, now)

    def update(t, d):
        cols = pl.ds(pl.multiple_of(d * WR, WR), WR)
        gain = jnp.where(flags[t], (upcoming * scale_s) * scale[:, cols], 0.0)
        fresh = base[:, cols] + gain * hfull[t, d].astype(f32)
        c[:, cols] = fresh
        cb[:, cols] = fresh.astype(bf16)

    for t in range(NMOVE):
        resid[t, me] = (outcome - jax.nn.sigmoid(tile)).astype(bf16)
        to_col(resid.at[t, me], resid.at[t, me], ssem.at[3 + t], rsem.at[3 + t])
        if t == 0:
            loglik_send(0, tile)
        landed(resid.at[t, pl.ds(0, NT - 1)], rsem.at[3 + t])

        whole = jnp.concatenate(
            [resid[t, p * NQ:(p + 1) * NQ].reshape(K, TP) for p in range(NZ)], axis=1
        )

        def shares(ds):
            block = jnp.concatenate(
                [xb[:, pl.ds(pl.multiple_of(d * WR, WR), WR)] for d in ds], axis=1
            )
            return jnp.dot(whole, block, preferred_element_type=f32).astype(bf16)

        order = row_ids + [rho]
        grad = shares(order[0:2])
        for g in range(0, NR, 2):
            ahead = shares(order[g + 2:g + 4]) if g + 2 < NR else None
            for j in range(2):
                i = g + j
                block = grad[:, j * WR:(j + 1) * WR]
                if i < NR - 1:
                    gsend[t, order[i]] = block
                    send(gsend.at[t, order[i]], grecv.at[t, rho], ssem.at[5 + t], rsem.at[5 + t], row_peers[i])
                else:
                    grecv[t, rho] = block
            grad = ahead
            if t == 0 and g == 0:
                loglik_over_col(0)
        if t == 0:
            landed(gm_got.at[pl.ds(0, NT - 1)], rsem.at[9])
            gm_all[me] = jnp.sum(gm_got[...], axis=0)
            to_col(gm_all.at[me], gm_all.at[me], ssem.at[14], rsem.at[14])
        else:
            free_part(t)

        landed(grecv.at[t, pl.ds(0, NR - 1)], rsem.at[5 + t])
        hfull[t, rho] = jnp.sum(grecv[t].astype(f32), axis=0).astype(bf16)
        for i, device in enumerate(row_peers):
            send(hfull.at[t, rho], hfull.at[t, rho], ssem.at[7 + t], hsem.at[t, i], device)

        if t == 0:
            row = loglik_total(0) * advance
            clipped = jnp.maximum(row - jnp.max(row), -CLIP_FLOOR)
            logw = clipped - jnp.log(jnp.sum(jnp.exp(clipped)))
            lw_ref[...] = logw
            weight = as_column(jnp.exp(logw))
            for d in range(NR):
                cols = pl.ds(d * WR, WR)
                block = c[:, cols]
                center = jnp.sum(weight * block, axis=0, keepdims=True)
                spread[:, cols] = jnp.sum(weight * (block - center) ** 2, axis=0, keepdims=True) + 1e-06
            landed(gm_all.at[pl.ds(0, NT - 1)], rsem.at[14])
            wide_sub = lax.broadcasted_iota(jnp.int32, (K, TP), 0)
            wide_lane = lax.rem(lax.broadcasted_iota(jnp.int32, (K, TP), 1), K)
            across = jnp.sum(jnp.where(wide_lane == wide_sub, weight, 0.0), axis=0, keepdims=True)
            term = weight * (jnp.where(wide_lane == wide_sub, 1.0, 0.0) - across)
            term = jnp.where(near, term[:K // 2], term[K // 2:])
            total = jnp.sum(term * gm_all[...].reshape(NT, TP)) + 1e-06 * P_SIZE
            scale[...] = stepped * (spread[...] / (total / P_SIZE))
            free_part(t)
        update(t, rho)
        for i in reversed(range(NR - 1)):
            landed(hfull.at[t, row_from[i]], hsem.at[t, i])
            update(t, row_from[i])
        tile = logits_phase(ps.at[t], rs.at[t], 1 + t)

    fin_pair[0] = loglik_row(tile)
    send(fin_pair.at[0], fin_pair.at[1], ssem.at[11], rsem.at[11], other)
    landed(fin_pair.at[1], rsem.at[11])
    fin_send[0] = fin_pair[0] + fin_pair[1]
    mine = (rho * NZ + z) * 2 + xl
    fin_all[mine] = fin_send[0]
    ys = [lax.rem(y + o, 4) for o in range(4)]
    xhs = [lax.rem(xh + o, 2) for o in range(2)]
    zz = [lax.rem(z + o, NZ) for o in range(NZ)]
    xls = [lax.rem(xl + o, 2) for o in range(2)]
    for dy, dx, dz, dl in ALL_OFFSETS:
        send(fin_send.at[0], fin_all.at[mine], ssem.at[13], rsem.at[13], (ys[dy], xhs[dx], zz[dz], xls[dl], co))
    landed(fin_all.at[pl.ds(0, NALL - 1)], rsem.at[13])
    ml_ref[...] = jnp.sum(fin_all[...], axis=0)[:, :K] / float(ROWS * NR)

    landed(pq, ssem.at[0])
    landed(rf.at[pl.ds(0, NT // 2 - 1)], ssem.at[15])
    for t in range(NMOVE):
        landed(ps.at[t, pl.ds(0, NT - 1)], ssem.at[1 + t])
        landed(resid.at[t, pl.ds(0, NT - 1)], ssem.at[3 + t])
        landed(gsend.at[t, pl.ds(0, NR - 1)], ssem.at[5 + t])
        landed(hfull.at[t, pl.ds(0, NR - 1)], ssem.at[7 + t])
    landed(ll_col.at[0, pl.ds(0, NT - 1)], ssem.at[10])
    landed(llr.at[0, pl.ds(0, NR - 1)], ssem.at[12])
    landed(fin_pair.at[1], ssem.at[11])
    landed(fin_all.at[pl.ds(0, NALL - 1)], ssem.at[13])
    landed(gm_got.at[pl.ds(0, NT - 1)], ssem.at[9])
    landed(gm_all.at[pl.ds(0, NT - 1)], ssem.at[14])


def finish(c_in, lw_in, ml_in, c_out, lw_out, ml_out, sem):
    copies = [
        pltpu.make_async_copy(src, dst, sem.at[i])
        for i, (src, dst) in enumerate(((ml_in, ml_out), (lw_in, lw_out), (c_in, c_out)))
    ]
    for copy in copies:
        copy.start()
    for copy in copies:
        copy.wait()


def local(doses, status, cloud, noise, flags, heat, advance, drift):
    f32, bf16 = jnp.float32, jnp.bfloat16
    vmem = pl.BlockSpec(memory_space=pltpu.VMEM)
    hbm = pl.BlockSpec(memory_space=pl.ANY)
    particles, logw, mean = pl.pallas_call(
        kernel,
        out_shape=(
            pltpu.VMEM((K, COLS), f32),
            pltpu.VMEM((1, K), f32),
            pltpu.VMEM((1, K), f32),
        ),
        in_specs=[hbm] * 8,
        out_specs=(vmem, vmem, vmem),
        scratch_shapes=[
            pltpu.VMEM((NZ, TP, COLS), jnp.int32),
            pltpu.VMEM((ROWS, COLS), bf16),
            pltpu.VMEM((NMOVE, K, COLS), f32),
            pltpu.VMEM((K, COLS), bf16),
            pltpu.VMEM((K, COLS), f32),
            pltpu.VMEM((1, COLS), f32),
            pltpu.VMEM((1, COLS), f32),
            pltpu.VMEM((NZ, TP), jnp.int32),
            pltpu.VMEM((NMOVE, K), jnp.int32),
            pltpu.SMEM((1,), f32),
            pltpu.SMEM((1,), f32),
            pltpu.SMEM((1,), f32),
            pltpu.VMEM((2, NZ, 2 * TK, TP), f32),
            pltpu.VMEM((NZ, 2 * TK, TP), f32),
            pltpu.VMEM((NZ, 2, TK, TP), f32),
            pltpu.VMEM((NT // 2, TK, TP), f32),
            pltpu.VMEM((NMOVE, NT, TK, TP), bf16),
            pltpu.VMEM((NMOVE, NT, TK, TP), bf16),
            pltpu.VMEM((NMOVE, NT, TK, TP), bf16),
            pltpu.VMEM((NMOVE, NR, K, WR), bf16),
            pltpu.VMEM((NMOVE, NR, K, WR), bf16),
            pltpu.VMEM((NMOVE, NR, K, WR), bf16),
            pltpu.VMEM((2, 1, TP), f32),
            pltpu.VMEM((1, 1, TP), f32),
            pltpu.VMEM((NALL, 1, TP), f32),
            pltpu.VMEM((1, 1, TP), f32),
            pltpu.VMEM((1, NT, 1, TP), f32),
            pltpu.VMEM((1, 1, TP), f32),
            pltpu.VMEM((1, NR, 1, TP), f32),
            pltpu.VMEM((NT, 1, TP), f32),
            pltpu.VMEM((NT, 1, TP), f32),
            pltpu.VMEM((NT, 1, TP), f32),
            pltpu.SemaphoreType.DMA((NZ,)),
            pltpu.SemaphoreType.DMA((7,)),
            pltpu.SemaphoreType.DMA((16,)),
            pltpu.SemaphoreType.DMA((15,)),
            pltpu.SemaphoreType.DMA((NMOVE, NR - 1)),
            pltpu.SemaphoreType.DMA((2,)),
        ],
        compiler_params=pltpu.CompilerParams(collective_id=0, has_side_effects=True),
    )(doses, status.reshape(NZ, TP), cloud, noise, flags, heat, advance, drift)
    particles, logw, mean = pl.pallas_call(
        finish,
        out_shape=(
            jax.ShapeDtypeStruct((K, COLS), f32),
            jax.ShapeDtypeStruct((1, K), f32),
            jax.ShapeDtypeStruct((1, K), f32),
        ),
        in_specs=[vmem] * 3,
        out_specs=(hbm, hbm, hbm),
        scratch_shapes=[pltpu.SemaphoreType.DMA((3,))],
        compiler_params=pltpu.CompilerParams(vmem_limit_bytes=1 << 20),
    )(particles, logw, mean)
    return particles, logw.reshape(K), mean.reshape(K)


def solution(mesh):
    torus = Mesh(mesh.devices.reshape(4, 2, 8, 2, 2), ("row_0", "row_1", "col_0", "col_1", "col_2"))
    return jax.shard_map(
        local,
        mesh=torus,
        in_specs=(P(ROW, COL), P(ROW), P(None, COL), P(None, None, COL), P(), P(), P(), P()),
        out_specs=(P(None, COL), P(), P()),
        check_vma=False,
    )
```

```python
import jax
import jax.numpy as jnp
from jax import lax
from jax.experimental import pallas as pl
from jax.experimental.pallas import tpu as pltpu
from jax.sharding import Mesh
from jax.sharding import PartitionSpec as P

P_SIZE = 65536
K = 64
ROW = ("row_0", "row_1")
COL = ("col_0", "col_1", "col_2")
CLIP_FLOOR = 4.0
SHRINKAGE_LEVEL = 0.5
MESH = pl.DeviceIdType.MESH

ROWS = 1024
COLS = 2048
NZ, NQ, NT, NR = 8, 4, 32, 8
TP = 128
TK = 16
WR = COLS // NR
NMOVE = 2
NALL = 128
ALL_OFFSETS = sorted(
    ((a, b, c, d) for a in range(4) for b in range(2) for c in range(8) for d in range(2) if a + b + c + d),
    key=lambda o: -(min(o[0], 4 - o[0]) + min(o[2], 8 - o[2]) + (0, 1, 2, 1)[2 * o[1] + o[3]]),
)
AHEAD = 4
Z_OFFSETS = (4, 3, 5, 2, 6, 1, 7, 0)
ROW_OFFSETS = ((2, 1), (1, 1), (3, 1), (2, 0), (0, 1), (1, 0), (3, 0))


def kernel(
    x_hbm, y_hbm, c_hbm, noise_hbm, flags_hbm, heat_hbm, adv_hbm, drift_hbm,
    c, lw_ref, ml_ref,
    xi, xb, noise, cb, base, spread, scale, y_ref, flags_ref, heat, adv, drift,
    pp, pq, pf, rf, ps, rs, resid, gsend, grecv, hfull,
    fin_pair, fin_send, fin_all, ll_send, ll_col, llr_send, llr, gm_send, gm_got, gm_all,
    xsem, lsem, ssem, rsem, hsem, psem,
):
    f32, bf16 = jnp.float32, jnp.bfloat16
    y, xh = lax.axis_index("row_0"), lax.axis_index("row_1")
    z, xl, co = lax.axis_index("col_0"), lax.axis_index("col_1"), lax.axis_index("col_2")
    q = co * 2 + xl
    me = z * NQ + q
    rho = y * 2 + xh
    scale_s = float(P_SIZE) ** (-0.5)
    zs = [lax.rem(z + o, NZ) for o in Z_OFFSETS]
    peers = [(zd, qd, (y, xh, zd, qd % 2, qd // 2)) for zd in zs[:-1] for qd in range(NQ)]
    for o in range(1, NQ):
        qd = lax.rem(q + o, NQ)
        peers.append((z, qd, (y, xh, z, lax.rem(qd, 2), qd // 2)))
    row_peers = [(lax.rem(y + o[0], 4), lax.rem(xh + o[1], 2), z, xl, co) for o in ROW_OFFSETS]
    row_ids = [p[0] * 2 + p[1] for p in row_peers]
    row_from = [lax.rem(y + 4 - o[0], 4) * 2 + lax.rem(xh + o[1], 2) for o in ROW_OFFSETS]

    def send(src, dst, send_at, recv_at, device):
        pltpu.make_async_remote_copy(
            src_ref=src, dst_ref=dst, send_sem=send_at, recv_sem=recv_at,
            device_id=device, device_id_type=MESH,
        ).start()

    def landed(ref, sem):
        pltpu.make_async_copy(ref, ref, sem).wait()

    def people(zd):
        return pl.ds(pl.multiple_of(zd * TP, TP), TP)

    copy_c = pltpu.make_async_copy(c_hbm, c, lsem.at[0])
    copy_c.start()
    x_copies = [
        pltpu.make_async_copy(x_hbm.at[people(zd)], xi.at[k], xsem.at[k]) for k, zd in enumerate(zs)
    ]

    for copy in x_copies[:AHEAD]:
        copy.start()

    barrier = pltpu.get_barrier_semaphore()
    for _, _, device in peers:
        pl.semaphore_signal(barrier, inc=1, device_id=device, device_id_type=MESH)
    for device in row_peers:
        pl.semaphore_signal(barrier, inc=1, device_id=device, device_id_type=MESH)

    small = [
        pltpu.make_async_copy(src, dst, lsem.at[1 + i])
        for i, (src, dst) in enumerate((
            (y_hbm, y_ref), (flags_hbm, flags_ref), (heat_hbm, heat), (adv_hbm, adv),
            (drift_hbm, drift), (noise_hbm, noise),
        ))
    ]

    def to_col(src, dst, send_at, recv_at):
        for _, _, device in peers:
            send(src, dst, send_at, recv_at, device)

    def to_row(src, dst, send_at, recv_at):
        for device in row_peers:
            send(src, dst, send_at, recv_at, device)

    def partial(zds):
        block = jnp.concatenate([xb[people(zd), :] for zd in zds], axis=0)
        return lax.dot_general(
            cb[...], block, (((1,), (1,)), ((), ())), preferred_element_type=f32
        )

    def collected(got, n, count):
        landed(got.at[pl.ds(0, count - 1)], rsem.at[n])
        return jnp.sum(got[...].astype(f32), axis=0) * scale_s

    def logits_phase(sent, got, n):
        groups = [(k, k + 1) for k in range(0, NZ, 2)]
        part = partial([zs[k] for k in groups[0]])
        for i, group in enumerate(groups):
            ahead = partial([zs[k] for k in groups[i + 1]]) if 0 < i < len(groups) - 1 else None
            for j, k in enumerate(group):
                for qd in range(NQ):
                    block = part[qd * TK:(qd + 1) * TK, j * TP:(j + 1) * TP]
                    sent[zs[k] * NQ + qd] = block.astype(sent.dtype)
                for zd, qd, device in peers[k * NQ:(k + 1) * NQ]:
                    send(sent.at[zd * NQ + qd], got.at[me], ssem.at[n], rsem.at[n], device)
            part = partial([zs[k] for k in groups[1]]) if i == 0 else ahead
        got[me] = sent[me]
        return collected(got, n, NT)

    def arrive(g):
        for k in (g, g + 1):
            x_copies[k].wait()
            if k + AHEAD < NZ:
                x_copies[k + AHEAD].start()

    def convert(g):
        for k in (g, g + 1):
            xb[people(zs[k]), :] = (xi[k].astype(f32) - 1.0).astype(bf16)

    def keep(g, part):
        for j in range(2):
            for h in range(2):
                pp[h, g + j] = part[h * 2 * TK:(h + 1) * 2 * TK, j * TP:(j + 1) * TP]

    half = NZ // 2
    other = (y, xh, z, xl, 1 - co)
    slot = z * 2 + xl

    def swap(g):
        ks = pl.ds(g * half, half)
        send(pp.at[1 - co, ks], pq.at[ks], ssem.at[0], psem.at[g], other)

    def joined(g):
        landed(pq.at[pl.ds(g * half, half)], psem.at[g])
        for k in range(g * half, (g + 1) * half):
            both = pp[co, k] + pq[k]
            for xd in range(2):
                pf[k, xd] = both[xd * TK:(xd + 1) * TK, :]
            if k < NZ - 1:
                for xd in range(2):
                    send(pf.at[k, xd], rf.at[slot], ssem.at[15], rsem.at[0], (y, xh, zs[k], xd, co))
            else:
                send(pf.at[k, 1 - xl], rf.at[slot], ssem.at[15], rsem.at[0], (y, xh, z, 1 - xl, co))
                rf[slot] = pf[k, xl]

    arrive(0)
    convert(0)
    copy_c.wait()
    cb[...] = c[...].astype(bf16)
    part = partial(zs[0:2])
    arrive(2)
    convert(2)
    keep(0, part)
    part = partial(zs[2:4])
    arrive(4)
    convert(4)
    keep(2, part)
    pl.semaphore_wait(barrier, NT - 1 + NR - 1)
    swap(0)
    part = partial(zs[4:6])
    arrive(6)
    convert(6)
    keep(4, part)
    joined(0)
    part = partial(zs[6:8])
    keep(6, part)
    swap(1)
    for copy in small:
        copy.start()
    joined(1)

    near = lax.broadcasted_iota(jnp.int32, (K // 2, TP), 1) < K
    gram = jnp.zeros((K, TP), f32)
    for d in range(NR):
        block = c[:, d * WR:(d + 1) * WR]
        block = block - jnp.mean(block, axis=0, keepdims=True)
        gram = gram + lax.dot_general(
            block, jnp.concatenate([block, block], axis=0), (((1,), (1,)), ((), ())),
            precision=lax.Precision.HIGHEST, preferred_element_type=f32,
        )
    folded = jnp.where(near, gram[:K // 2], gram[K // 2:])
    for d in range(NT):
        gm_send[d] = folded[d:d + 1, :]
    for zd, qd, device in peers:
        send(gm_send.at[zd * NQ + qd], gm_got.at[me], ssem.at[9], rsem.at[9], device)
    gm_got[me] = gm_send[me]

    for copy in small:
        copy.wait()
    outcome = y_ref[pl.ds(z, 1), :].astype(f32)
    sub = lax.broadcasted_iota(jnp.int32, (TK, TP), 0)
    lane = lax.broadcasted_iota(jnp.int32, (TK, TP), 1)

    def loglik_row(tile):
        soft = jnp.maximum(tile, 0.0) + jnp.log1p(jnp.exp(-jnp.abs(tile)))
        total = jnp.sum(outcome * tile - soft, axis=1, keepdims=True)
        return jnp.sum(jnp.where(lane == sub + q * TK, total, 0.0), axis=0, keepdims=True)

    eye = lax.broadcasted_iota(jnp.int32, (K, K), 0) == lax.broadcasted_iota(jnp.int32, (K, K), 1)

    def as_column(row):
        return jnp.sum(jnp.where(eye, row, 0.0), axis=1, keepdims=True)

    flags = [as_column(flags_ref[t:t + 1, :].astype(f32)) > 0.5 for t in range(NMOVE)]
    advance = adv[0]
    stepped = drift[0]
    upcoming = heat[0] + advance

    tile = collected(rf, 0, NT // 2)

    def loglik_send(u, tile):
        ll_send[u] = loglik_row(tile)
        ll_col[u, me] = ll_send[u]
        to_col(ll_send.at[u], ll_col.at[u, me], ssem.at[10 + u], rsem.at[10 + u])

    def loglik_over_col(u):
        landed(ll_col.at[u, pl.ds(0, NT - 1)], rsem.at[10 + u])
        llr_send[u] = jnp.sum(ll_col[u], axis=0)
        llr[u, rho] = llr_send[u]
        to_row(llr_send.at[u], llr.at[u, rho], ssem.at[12 + u], rsem.at[12 + u])

    def loglik_total(u):
        landed(llr.at[u, pl.ds(0, NR - 1)], rsem.at[12 + u])
        return jnp.sum(llr[u], axis=0)[:, :K]

    def free_part(t):
        for d in range(NR):
            cols = pl.ds(d * WR, WR)
            now = c[:, cols]
            a = scale[:, cols]
            pull = now / jnp.sqrt(now * now + 1.0)
            moved = now - (SHRINKAGE_LEVEL * a) * pull + jnp.sqrt(2.0 * a) * noise[t, :, cols]
            base[:, cols] = jnp.where(flags[t], moved, now)

    def update(t, d):
        cols = pl.ds(pl.multiple_of(d * WR, WR), WR)
        gain = jnp.where(flags[t], (upcoming * scale_s) * scale[:, cols], 0.0)
        fresh = base[:, cols] + gain * hfull[t, d].astype(f32)
        c[:, cols] = fresh
        cb[:, cols] = fresh.astype(bf16)

    for t in range(NMOVE):
        resid[t, me] = (outcome - jax.nn.sigmoid(tile)).astype(bf16)
        to_col(resid.at[t, me], resid.at[t, me], ssem.at[3 + t], rsem.at[3 + t])
        if t == 0:
            loglik_send(0, tile)
        landed(resid.at[t, pl.ds(0, NT - 1)], rsem.at[3 + t])

        whole = jnp.concatenate(
            [resid[t, p * NQ:(p + 1) * NQ].reshape(K, TP) for p in range(NZ)], axis=1
        )

        def shares(ds):
            block = jnp.concatenate(
                [xb[:, pl.ds(pl.multiple_of(d * WR, WR), WR)] for d in ds], axis=1
            )
            return jnp.dot(whole, block, preferred_element_type=f32).astype(bf16)

        order = row_ids + [rho]
        grad = shares(order[0:2])
        for g in range(0, NR, 2):
            ahead = shares(order[g + 2:g + 4]) if 0 < g < NR - 2 else None
            for j in range(2):
                i = g + j
                block = grad[:, j * WR:(j + 1) * WR]
                if i < NR - 1:
                    gsend[t, order[i]] = block
                    send(gsend.at[t, order[i]], grecv.at[t, rho], ssem.at[5 + t], rsem.at[5 + t], row_peers[i])
                else:
                    grecv[t, rho] = block
            grad = shares(order[2:4]) if g == 0 else ahead
            if t == 0 and g == 0:
                loglik_over_col(0)
        if t == 0:
            landed(gm_got.at[pl.ds(0, NT - 1)], rsem.at[9])
            gm_all[me] = jnp.sum(gm_got[...], axis=0)
            to_col(gm_all.at[me], gm_all.at[me], ssem.at[14], rsem.at[14])
        else:
            free_part(t)

        landed(grecv.at[t, pl.ds(0, NR - 1)], rsem.at[5 + t])
        hfull[t, rho] = jnp.sum(grecv[t].astype(f32), axis=0).astype(bf16)
        for i, device in enumerate(row_peers):
            send(hfull.at[t, rho], hfull.at[t, rho], ssem.at[7 + t], hsem.at[t, i], device)

        if t == 0:
            row = loglik_total(0) * advance
            clipped = jnp.maximum(row - jnp.max(row), -CLIP_FLOOR)
            logw = clipped - jnp.log(jnp.sum(jnp.exp(clipped)))
            lw_ref[...] = logw
            weight = as_column(jnp.exp(logw))
            for d in range(NR):
                cols = pl.ds(d * WR, WR)
                block = c[:, cols]
                center = jnp.sum(weight * block, axis=0, keepdims=True)
                spread[:, cols] = jnp.sum(weight * (block - center) ** 2, axis=0, keepdims=True) + 1e-06
            landed(gm_all.at[pl.ds(0, NT - 1)], rsem.at[14])
            wide_sub = lax.broadcasted_iota(jnp.int32, (K, TP), 0)
            wide_lane = lax.rem(lax.broadcasted_iota(jnp.int32, (K, TP), 1), K)
            across = jnp.sum(jnp.where(wide_lane == wide_sub, weight, 0.0), axis=0, keepdims=True)
            term = weight * (jnp.where(wide_lane == wide_sub, 1.0, 0.0) - across)
            term = jnp.where(near, term[:K // 2], term[K // 2:])
            total = jnp.sum(term * gm_all[...].reshape(NT, TP)) + 1e-06 * P_SIZE
            scale[...] = stepped * (spread[...] / (total / P_SIZE))
            free_part(t)
        update(t, rho)
        for i in reversed(range(NR - 1)):
            landed(hfull.at[t, row_from[i]], hsem.at[t, i])
            update(t, row_from[i])
        tile = logits_phase(ps.at[t], rs.at[t], 1 + t)

    fin_pair[0] = loglik_row(tile)
    send(fin_pair.at[0], fin_pair.at[1], ssem.at[11], rsem.at[11], other)
    landed(fin_pair.at[1], rsem.at[11])
    fin_send[0] = fin_pair[0] + fin_pair[1]
    mine = (rho * NZ + z) * 2 + xl
    fin_all[mine] = fin_send[0]
    ys = [lax.rem(y + o, 4) for o in range(4)]
    xhs = [lax.rem(xh + o, 2) for o in range(2)]
    zz = [lax.rem(z + o, NZ) for o in range(NZ)]
    xls = [lax.rem(xl + o, 2) for o in range(2)]
    for dy, dx, dz, dl in ALL_OFFSETS:
        send(fin_send.at[0], fin_all.at[mine], ssem.at[13], rsem.at[13], (ys[dy], xhs[dx], zz[dz], xls[dl], co))
    landed(fin_all.at[pl.ds(0, NALL - 1)], rsem.at[13])
    ml_ref[...] = jnp.sum(fin_all[...], axis=0)[:, :K] / float(ROWS * NR)

    landed(pq, ssem.at[0])
    landed(rf.at[pl.ds(0, NT // 2 - 1)], ssem.at[15])
    for t in range(NMOVE):
        landed(ps.at[t, pl.ds(0, NT - 1)], ssem.at[1 + t])
        landed(resid.at[t, pl.ds(0, NT - 1)], ssem.at[3 + t])
        landed(gsend.at[t, pl.ds(0, NR - 1)], ssem.at[5 + t])
        landed(hfull.at[t, pl.ds(0, NR - 1)], ssem.at[7 + t])
    landed(ll_col.at[0, pl.ds(0, NT - 1)], ssem.at[10])
    landed(llr.at[0, pl.ds(0, NR - 1)], ssem.at[12])
    landed(fin_pair.at[1], ssem.at[11])
    landed(fin_all.at[pl.ds(0, NALL - 1)], ssem.at[13])
    landed(gm_got.at[pl.ds(0, NT - 1)], ssem.at[9])
    landed(gm_all.at[pl.ds(0, NT - 1)], ssem.at[14])


def finish(c_in, lw_in, ml_in, c_out, lw_out, ml_out, sem):
    copies = [
        pltpu.make_async_copy(src, dst, sem.at[i])
        for i, (src, dst) in enumerate(((ml_in, ml_out), (lw_in, lw_out), (c_in, c_out)))
    ]
    for copy in copies:
        copy.start()
    for copy in copies:
        copy.wait()


def local(doses, status, cloud, noise, flags, heat, advance, drift):
    f32, bf16 = jnp.float32, jnp.bfloat16
    vmem = pl.BlockSpec(memory_space=pltpu.VMEM)
    hbm = pl.BlockSpec(memory_space=pl.ANY)
    particles, logw, mean = pl.pallas_call(
        kernel,
        out_shape=(
            pltpu.VMEM((K, COLS), f32),
            pltpu.VMEM((1, K), f32),
            pltpu.VMEM((1, K), f32),
        ),
        in_specs=[hbm] * 8,
        out_specs=(vmem, vmem, vmem),
        scratch_shapes=[
            pltpu.VMEM((NZ, TP, COLS), jnp.int32),
            pltpu.VMEM((ROWS, COLS), bf16),
            pltpu.VMEM((NMOVE, K, COLS), f32),
            pltpu.VMEM((K, COLS), bf16),
            pltpu.VMEM((K, COLS), f32),
            pltpu.VMEM((1, COLS), f32),
            pltpu.VMEM((1, COLS), f32),
            pltpu.VMEM((NZ, TP), jnp.int32),
            pltpu.VMEM((NMOVE, K), jnp.int32),
            pltpu.SMEM((1,), f32),
            pltpu.SMEM((1,), f32),
            pltpu.SMEM((1,), f32),
            pltpu.VMEM((2, NZ, 2 * TK, TP), f32),
            pltpu.VMEM((NZ, 2 * TK, TP), f32),
            pltpu.VMEM((NZ, 2, TK, TP), f32),
            pltpu.VMEM((NT // 2, TK, TP), f32),
            pltpu.VMEM((NMOVE, NT, TK, TP), bf16),
            pltpu.VMEM((NMOVE, NT, TK, TP), bf16),
            pltpu.VMEM((NMOVE, NT, TK, TP), bf16),
            pltpu.VMEM((NMOVE, NR, K, WR), bf16),
            pltpu.VMEM((NMOVE, NR, K, WR), bf16),
            pltpu.VMEM((NMOVE, NR, K, WR), bf16),
            pltpu.VMEM((2, 1, TP), f32),
            pltpu.VMEM((1, 1, TP), f32),
            pltpu.VMEM((NALL, 1, TP), f32),
            pltpu.VMEM((1, 1, TP), f32),
            pltpu.VMEM((1, NT, 1, TP), f32),
            pltpu.VMEM((1, 1, TP), f32),
            pltpu.VMEM((1, NR, 1, TP), f32),
            pltpu.VMEM((NT, 1, TP), f32),
            pltpu.VMEM((NT, 1, TP), f32),
            pltpu.VMEM((NT, 1, TP), f32),
            pltpu.SemaphoreType.DMA((NZ,)),
            pltpu.SemaphoreType.DMA((7,)),
            pltpu.SemaphoreType.DMA((16,)),
            pltpu.SemaphoreType.DMA((15,)),
            pltpu.SemaphoreType.DMA((NMOVE, NR - 1)),
            pltpu.SemaphoreType.DMA((2,)),
        ],
        compiler_params=pltpu.CompilerParams(collective_id=0, has_side_effects=True),
    )(doses, status.reshape(NZ, TP), cloud, noise, flags, heat, advance, drift)
    particles, logw, mean = pl.pallas_call(
        finish,
        out_shape=(
            jax.ShapeDtypeStruct((K, COLS), f32),
            jax.ShapeDtypeStruct((1, K), f32),
            jax.ShapeDtypeStruct((1, K), f32),
        ),
        in_specs=[vmem] * 3,
        out_specs=(hbm, hbm, hbm),
        scratch_shapes=[pltpu.SemaphoreType.DMA((3,))],
        compiler_params=pltpu.CompilerParams(vmem_limit_bytes=1 << 20),
    )(particles, logw, mean)
    return particles, logw.reshape(K), mean.reshape(K)


def solution(mesh):
    torus = Mesh(mesh.devices.reshape(4, 2, 8, 2, 2), ("row_0", "row_1", "col_0", "col_1", "col_2"))
    return jax.shard_map(
        local,
        mesh=torus,
        in_specs=(P(ROW, COL), P(ROW), P(None, COL), P(None, None, COL), P(), P(), P(), P()),
        out_specs=(P(None, COL), P(), P()),
        check_vma=False,
    )
```
